32 devices in a mesh: dp: 8 (over z, y), mp: 4 (over x, core).
Axes of the slice: x: 2, y: 2, z: 4, core: 2. Of those that a mesh axis runs over, the one named last changes fastest.
Arguments:
- tokens: bfloat16 [16384, 768], P(('dp', 'mp')), may hold values from -6 to 6
- cotangent: bfloat16 [16384, 768], P(('dp', 'mp')), may hold values from -6 to 6
- norm1_gain: float32 [768], replicated, may hold values from 0.5 to 1.5
- w_query: bfloat16 [768, 768], P(None, 'mp'), may hold values from -0.21875 to 0.21875
- w_key: bfloat16 [768, 768], P(None, 'mp'), may hold values from -0.21875 to 0.21875
- w_value: bfloat16 [768, 768], P(None, 'mp'), may hold values from -0.21875 to 0.21875
- w_attn_out: bfloat16 [768, 768], P('mp'), may hold values from -1.796875 to 1.796875
- bias_table: float32 [32, 12], P(None, 'mp'), may hold values from -6 to 6
- norm2_gain: float32 [768], replicated, may hold values from 0.5 to 1.5
- w_router: bfloat16 [768, 64], replicated, may hold values from -0.109375 to 0.109375
- w_expert_in: bfloat16 [64, 768, 3072], P('dp', None, 'mp'), may hold values from -0.21875 to 0.21875
- w_expert_out: bfloat16 [64, 3072, 768], P('dp', 'mp'), may hold values from -18 to 18
- routes: int32 [16384, 1], P(('dp', 'mp')), may hold values from 0 to 63; in each aligned block of 512 rows (0 to 511, 512 to 1023, ...) at most 16 rows name the same one
- segments: int32 [8, 2048], P('dp'), may hold values from 0 to 7, never falling along the last dimension, each value on 1 to 1024 neighbouring positions
- buckets: int32 [4095], replicated, may hold values from 0 to 31
Outputs:
- mixed: bfloat16 [16384, 768], P(('dp', 'mp'))
- grad_tokens: bfloat16 [16384, 768], P(('dp', 'mp'))
- grad_norm1_gain: float32 [768], replicated
- grad_w_query: float32 [768, 768], P(None, 'mp')
- grad_w_key: float32 [768, 768], P(None, 'mp')
- grad_w_value: float32 [768, 768], P(None, 'mp')
- grad_w_attn_out: float32 [768, 768], P('mp')
- grad_bias_table: float32 [32, 12], P(None, 'mp')
- grad_norm2_gain: float32 [768], replicated
- grad_w_router: float32 [768, 64], replicated
- grad_w_expert_in: float32 [64, 768, 3072], P('dp', None, 'mp')
- grad_w_expert_out: float32 [64, 3072, 768], P('dp', 'mp')
The draws below stay inside these ranges and needn't reach their ends.
Inputs may be any that keep to these rules, and one draw needn't show every extreme that they name: `routes`: among the 512 rows of one device at most 16 name the same expert, and in every draw some expert is named by exactly 16 rows of some device. `segments`: within a sequence the document numbers never fall; each document has 1 to 1024 positions, one exactly that many.
All inputs are finite; a program needn't handle non-finite values.
Results may differ from the reference program's by a relative error of at most 0.018.
Values may be sent and summed in bfloat16 or wider, within the bound.
No kernel may reach another device: no remote copies, remote signals or barrier semaphores. Data moves between devices by JAX's collectives and lax.ppermute only.
A program may use at most 256 MiB of HBM per device.

```python
import math
import jax
import jax.numpy as jnp
import numpy as np
from jax import lax

D = 768
HEADS = 12
HEAD_DIM = 64
FF = 3072
EXPERTS = 64
BUCKETS = 32
TOK_DEV = 512
SEQ = 2048
TOKENS = 16384
CAP = 16
N_DP = 8
N_MP = 4


def touch_ends(array, rng, smallest, top_value):
    longest = array.shape.index(max(array.shape))
    spots = []
    for shift in (0, 1):
        where = [jax.random.randint(jax.random.fold_in(rng, axis), (), 0, length) for axis, length in enumerate(array.shape)]
        where[longest] = (where[longest] + shift) % array.shape[longest]
        spots.append(tuple(where))
    return array.at[spots[0]].set(smallest).at[spots[1]].set(top_value)


def steps_of(own_key, shape, shards, smallest, high):
    factor_of = 1.0
    for dim, shards_of in shards:
        heights = jax.random.uniform(jax.random.fold_in(jax.random.fold_in(own_key, 6), dim), (shards_of,), jnp.float32, smallest / len(shards), high / len(shards))
        factor_of = factor_of * jnp.repeat(jnp.exp(heights), shape[dim] // shards_of).reshape((-1,) + (1,) * (len(shape) - 1 - dim))
    return factor_of


def profile(count, total, limit, skew):
    loads = [(1 << 20) // math.isqrt(grade ** skew) + 1 for grade in range(2, count + 1)]
    spare, counts = total - limit - (count - 1), [1] * (count - 1)
    while spare > 0:
        candidates = [i for i in range(count - 1) if counts[i] < limit]
        mass, left = sum([loads[i] for i in candidates]), spare
        for i in candidates:
            extra = min(limit - counts[i], max(1, left * loads[i] // mass), spare)
            counts[i] = counts[i] + extra
            spare = spare - extra
    return np.array([limit] + counts)


def uneven(rng, amount, total, bound, slope):
    if amount == 2:
        one = jax.random.randint(rng, (), max(1, total - bound), min(bound, total - 1) + 1)
        return jnp.stack([one, total - one])
    tallies = jnp.asarray(profile(amount, total, bound, slope), jnp.int32)
    couples = (amount - 1) // 2
    giver, receiver = tallies[1:1 + 2 * couples:2], tallies[2:2 + 2 * couples:2]
    room = jnp.minimum(giver - 1, bound - receiver)
    moved = jax.random.randint(jax.random.fold_in(rng, 1), (couples,), 0, 1 << 20) % (room + 1)
    tallies = tallies.at[1:1 + 2 * couples:2].set(giver - moved).at[2:2 + 2 * couples:2].set(receiver + moved)
    return tallies[jax.random.permutation(jax.random.fold_in(rng, 2), amount)]


def shared_out(rng, own, number, rows, amount, top, most, skew):
    ranking = jax.random.permutation(rng, amount)
    packed, ordinary = load_shares(amount, rows * top, most, skew, True), load_shares(amount, rows * top, most, skew, False)
    places = jnp.arange(amount)

    def named(lengths, offset_by):
        used = int((lengths > 0).sum())
        fixed = max(1, used // 4)
        passed = fixed + (places - fixed + offset_by * (used - fixed)) % max(1, amount - fixed)
        return jnp.zeros((amount,), jnp.int32).at[ranking[jnp.where(places < fixed, places, passed)]].set(jnp.asarray(lengths, jnp.int32))

    lengths = jnp.where(number % 4 == 0, named(packed, number // 4), named(ordinary, number - number // 4 - 1))
    mixed = jax.random.permutation(jax.random.fold_in(own, 3), amount)
    donor, receiver = mixed[0:amount // 2 * 2:2], mixed[1:amount // 2 * 2:2]
    slack = jnp.minimum(lengths[donor] - 1, most - lengths[receiver]) // 2
    slack = jnp.where((donor == ranking[0]) | (receiver == ranking[0]) | (lengths[receiver] == 0), 0, jnp.maximum(slack, 0))
    passed = jax.random.randint(jax.random.fold_in(own, 4), (amount // 2,), 0, 1 << 20) % (slack + 1)
    lengths = lengths.at[donor].add(-passed).at[receiver].add(passed)
    items = jnp.searchsorted(jnp.cumsum(lengths), jnp.arange(rows * top), side="right").astype(jnp.int32)
    listing = items.reshape(top, rows).T
    listing = listing[jax.random.permutation(jax.random.fold_in(own, 1), rows)]
    offset_by = jax.random.randint(jax.random.fold_in(own, 2), (rows, 1), 0, top)
    return jnp.take_along_axis(listing, (jnp.arange(top)[None, :] + offset_by) % top, axis=1)


def load_shares(count, total, limit, skew, full):
    weights = [(1 << 20) // math.isqrt(grade ** skew) + 1 for grade in range(1, count + 1)]
    largest = limit if full else min(limit, max(-(-total // count), total * weights[0] // sum(weights)))
    least = 1 if total - largest >= count - 1 else 0
    counts, surplus = [largest] + [least] * (count - 1), total - largest - least * (count - 1)
    while surplus > 0:
        movable = [i for i in range(1, count) if counts[i] < largest] or [i for i in range(1, count) if counts[i] < limit]
        whole, remaining = sum([weights[i] for i in movable]), surplus
        for i in movable:
            more = min(limit - counts[i], max(1, remaining * weights[i] // whole), surplus)
            counts[i] = counts[i] + more
            surplus = surplus - more
    return np.array(counts)


def gaussian(rng, dims, spread, reach, shards=(), held_as=jnp.bfloat16):
    values = jax.random.normal(rng, dims, jnp.float32) * spread
    if len(shards) > 0:
        values = steps_of(rng, dims, shards, -0.22, 0.18) * values
    return jnp.clip(values, min=-reach, max=reach).astype(held_as)


def setup_inputs(seed: int = 0) -> dict:
    seeds = jax.random.split(jax.random.key(seed), 16)
    tokens = gaussian(seeds[0], (TOKENS, D), 1.0, 6.0, ((0, 32),))
    cotangent = gaussian(seeds[1], (TOKENS, D), 1.0, 6.0, ((0, 32),))
    norm1_gain = jnp.clip(1.0 + 0.1 * jax.random.normal(seeds[2], (D,), jnp.float32), 0.5, 1.5)
    w_query = gaussian(seeds[3], (D, D), D ** -0.5, 0.21875, ((1, 4),))
    w_key = gaussian(seeds[4], (D, D), D ** -0.5, 0.21875, ((1, 4),))
    w_value = gaussian(seeds[5], (D, D), D ** -0.5, 0.21875, ((1, 4),))
    w_attn_out = gaussian(seeds[6], (D, D), 0.3, 1.796875, ((0, 4),))
    bias_table = gaussian(seeds[7], (BUCKETS, HEADS), 1.0, 6.0, ((1, 4),), jnp.float32)
    norm2_gain = jnp.clip(1.0 + 0.1 * jax.random.normal(seeds[8], (D,), jnp.float32), 0.5, 1.5)
    w_router = gaussian(seeds[9], (D, EXPERTS), (4 * D) ** -0.5, 0.109375)
    w_expert_in = gaussian(seeds[10], (EXPERTS, D, FF), D ** -0.5, 0.21875, ((0, 8), (2, 4)))
    w_expert_out = gaussian(seeds[11], (EXPERTS, FF, D), 3.0, 18.0, ((0, 8), (1, 4)))
    routes_keys = jax.random.split(jax.random.fold_in(seeds[12], 1), TOKENS // TOK_DEV)
    routes_turns = jax.random.permutation(jax.random.fold_in(seeds[12], 3), TOKENS // TOK_DEV)
    routes = jax.vmap(lambda own, number: shared_out(jax.random.fold_in(seeds[12], 2), own, number, TOK_DEV, EXPERTS, 1, CAP, 1))(routes_keys, routes_turns).reshape((TOKENS, 1))
    segments = jax.vmap(lambda own: jnp.searchsorted(jnp.cumsum(uneven(own, 8, SEQ, SEQ // 2, 1)), jnp.arange(SEQ), side="right"))(jax.random.split(seeds[13], N_DP)).reshape((N_DP, SEQ)).astype(jnp.int32)
    buckets = touch_ends(jax.random.randint(seeds[14], (2 * SEQ - 1,), 0, BUCKETS), jax.random.fold_in(seeds[14], 1), 0, BUCKETS - 1).astype(jnp.int32)
    return {"tokens": tokens, "cotangent": cotangent, "norm1_gain": norm1_gain, "w_query": w_query, "w_key": w_key, "w_value": w_value, "w_attn_out": w_attn_out, "bias_table": bias_table, "norm2_gain": norm2_gain, "w_router": w_router, "w_expert_in": w_expert_in, "w_expert_out": w_expert_out, "routes": routes, "segments": segments, "buckets": buckets}


@jax.custom_vjp
def low(v):
    return lax.optimization_barrier(v.astype(jnp.bfloat16)).astype(jnp.float32)

@jax.custom_vjp
def low_back(v):
    return v

def low_keep(v):
    return (low(v), None)

def low_pass(kept, grad):
    return (grad,)

def back_keep(v):
    return (v, None)

def back_low(kept, grad):
    return (low(grad),)
low.defvjp(low_keep, low_pass)
low_back.defvjp(back_keep, back_low)
EPSILON = 1e-06
SCORE_SCALE = 0.125
MASKED = -1e+30
PRECISE = lax.Precision.HIGHEST

def rms_norm(values, gain):
    return values * lax.rsqrt(lax.optimization_barrier(jnp.mean(values * values, axis=-1, keepdims=True)) + EPSILON) * gain

def matmul_high(left, right):
    return jnp.dot(left, right, precision=PRECISE)

def attention_rows(query_heads, key_heads, value_heads, bias_grid, buckets, seg_row, block_rows, row_start):
    query_rows = lax.dynamic_slice_in_dim(query_heads, row_start, block_rows, 0)
    raw_scores = low_back(jnp.einsum('rhd,lhd->hrl', query_rows, key_heads, precision=PRECISE) * SCORE_SCALE)
    positions = (row_start + jnp.arange(block_rows).astype(jnp.int32)).astype(jnp.int32)
    offsets = (jnp.arange(SEQ).astype(jnp.int32)[None, :] - positions[:, None] + SEQ - 1).astype(jnp.int32)
    bias_rows = jnp.transpose(bias_grid[buckets[offsets]], (2, 0, 1))
    seg_rows = lax.dynamic_slice_in_dim(seg_row, row_start, block_rows, 0)
    same_doc = seg_rows[:, None] == seg_row[None, :]
    logits = jnp.where(same_doc[None], raw_scores + bias_rows, MASKED)
    row_max = lax.optimization_barrier(jnp.max(logits, axis=-1, keepdims=True))
    exp_scores = jnp.exp(logits - row_max)
    weights = low(exp_scores / lax.optimization_barrier(jnp.sum(exp_scores, axis=-1, keepdims=True)))
    return jnp.einsum('hrl,lhd->rhd', weights, value_heads, precision=PRECISE)

def reference(tokens, cotangent, norm1_gain, w_query, w_key, w_value, w_attn_out, bias_table, norm2_gain, w_router, w_expert_in, w_expert_out, routes, segments, buckets):
    block_rows = min(512, SEQ)
    sources = N_DP * N_MP
    expert_of = routes[:, 0].astype(jnp.int32)
    member = (expert_of.reshape(sources, TOK_DEV)[:, :, None] == jnp.arange(EXPERTS).astype(jnp.int32)[None, None, :]).astype(jnp.int32)
    slot_rank = lax.optimization_barrier(jnp.sum((jnp.cumsum(member, axis=1).astype(jnp.int32) - 1) * member, axis=-1)).astype(jnp.int32).reshape(TOKENS)
    source_of = (jnp.arange(TOKENS).astype(jnp.int32) // TOK_DEV).astype(jnp.int32)
    slot_index = (expert_of * (sources * CAP) + source_of * CAP + slot_rank).astype(jnp.int32)
    slot_table = jnp.full((EXPERTS * sources * CAP,), TOKENS, jnp.int32).at[slot_index].set(jnp.arange(TOKENS).astype(jnp.int32))
    chosen = (expert_of[:, None] == jnp.arange(EXPERTS).astype(jnp.int32)[None, :]).astype(jnp.float32)
    starts = (jnp.arange(SEQ // block_rows) * block_rows).astype(jnp.int32)

    def forward(inputs, gain_one, query_weight, key_weight, value_weight, out_weight, bias_grid, gain_two, router_weight, expert_in, expert_out):
        normed_one = low(rms_norm(inputs, gain_one))

        def one_sequence(carried, item_pair):
            normed, seg_row = item_pair
            query_heads = low(low_back(matmul_high(normed, query_weight))).reshape(SEQ, HEADS, HEAD_DIM)
            key_heads = low(low_back(matmul_high(normed, key_weight))).reshape(SEQ, HEADS, HEAD_DIM)
            value_heads = low(low_back(matmul_high(normed, value_weight))).reshape(SEQ, HEADS, HEAD_DIM)

            def rows_of(row_start):
                return attention_rows(query_heads, key_heads, value_heads, bias_grid, buckets, seg_row, block_rows, row_start)
            head_out = lax.map(jax.checkpoint(rows_of), starts)
            head_out = low(low_back(head_out.reshape(SEQ, D)))
            return (carried, matmul_high(head_out, out_weight))
        _, attn = lax.scan(one_sequence, jnp.zeros((), jnp.float32), (normed_one.reshape(N_DP, SEQ, D), segments))
        hidden = inputs + low_back(attn.reshape(TOKENS, D))
        normed_two = low(rms_norm(hidden, gain_two))
        router_probs = jax.nn.softmax(matmul_high(normed_two, router_weight), axis=-1)
        gate_prob = lax.optimization_barrier(jnp.sum(router_probs * chosen, axis=-1, keepdims=True))
        padded = jnp.concatenate([normed_two, jnp.zeros((1, D), jnp.float32)], axis=0)
        slot_rows = padded[slot_table].reshape(EXPERTS, sources * CAP, D)
        pre_act = low_back(jnp.einsum('erd,edf->erf', slot_rows, expert_in, precision=PRECISE))
        activated = low(jax.nn.gelu(pre_act, approximate=True))
        slot_out = jnp.einsum('erf,efd->erd', activated, expert_out, precision=PRECISE).reshape(EXPERTS * sources * CAP, D)
        expert_rows = slot_out[slot_index]
        return hidden + gate_prob * low_back(expert_rows)
    mixed, pullback = jax.vjp(forward, tokens.astype(jnp.float32), norm1_gain, w_query.astype(jnp.float32), w_key.astype(jnp.float32), w_value.astype(jnp.float32), w_attn_out.astype(jnp.float32), bias_table, norm2_gain, w_router.astype(jnp.float32), w_expert_in.astype(jnp.float32), w_expert_out.astype(jnp.float32))
    grads = pullback(cotangent.astype(jnp.float32))
    return (mixed.astype(jnp.bfloat16), grads[0].astype(jnp.bfloat16), grads[1], grads[2], grads[3], grads[4], grads[5], grads[6], grads[7], grads[8], grads[9], grads[10])
```

```python
import jax
import jax.numpy as jnp
from jax import lax
from jax.sharding import PartitionSpec as P

EPSILON = 1e-06
SCORE_SCALE = 0.125
MASKED = -1e30
PRECISE = lax.Precision.HIGHEST


def rms_scale(values):
    return lax.rsqrt(jnp.mean(values * values, axis=-1, keepdims=True) + EPSILON)


def norm_back(values, scale, gain, upstream):
    weighted = gain * upstream
    gain_grad = jnp.sum(upstream * values * scale, axis=0)
    input_grad = scale * weighted - values * scale * scale * scale * jnp.mean(
        weighted * values, axis=-1, keepdims=True
    )
    return (input_grad, gain_grad)


def gelu_tanh(values):
    return jax.nn.gelu(values, approximate=True)


def band_block(bias_rows, row_start, block_rows, seq_length):
    head_count = bias_rows.shape[0]
    width = seq_length + block_rows - 1
    window = lax.dynamic_slice_in_dim(bias_rows, seq_length - row_start - block_rows, width, 1)
    repeated = jnp.broadcast_to(window[:, None, :], (head_count, block_rows, width)).reshape(
        head_count, block_rows * width
    )
    repeated = jnp.pad(repeated, ((0, 0), (0, block_rows)))
    return repeated.reshape(head_count, block_rows, width + 1)[:, ::-1, :seq_length]


def band_sums(grad_block, block_rows, seq_length):
    head_count = grad_block.shape[0]
    width = seq_length + block_rows - 1
    flipped = grad_block[:, ::-1, :]
    padded = jnp.pad(flipped, ((0, 0), (0, 0), (0, block_rows))).reshape(
        head_count, block_rows * (seq_length + block_rows)
    )
    skewed = padded[:, : block_rows * width].reshape(head_count, block_rows, width)
    return jnp.sum(skewed, axis=1)


def score_block(query_rows, key_heads, bias_rows, seg_rows, seg_all, row_start, block_rows):
    seq_length = key_heads.shape[0]
    raw_scores = (
        jnp.einsum("rhd,lhd->hrl", query_rows, key_heads, preferred_element_type=jnp.float32)
        * SCORE_SCALE
    )
    logits = raw_scores + band_block(bias_rows, row_start, block_rows, seq_length)
    same_doc = seg_rows[:, None] == seg_all[None, :]
    return jnp.where(same_doc[None], logits, MASKED)


def attend(query_heads, key_heads, value_heads, bias_rows, seg_all, block_rows):
    seq_length = key_heads.shape[0]
    starts = jnp.arange(seq_length // block_rows, dtype=jnp.int32) * block_rows

    def one_block(row_start):
        query_rows = lax.dynamic_slice_in_dim(query_heads, row_start, block_rows, 0)
        seg_rows = lax.dynamic_slice_in_dim(seg_all, row_start, block_rows, 0)
        logits = score_block(
            query_rows, key_heads, bias_rows, seg_rows, seg_all, row_start, block_rows
        )
        row_max = jnp.max(logits, axis=-1, keepdims=True)
        exp_scores = jnp.exp(logits - row_max)
        row_total = jnp.sum(exp_scores, axis=-1, keepdims=True)
        weights = (exp_scores / row_total).astype(jnp.bfloat16)
        head_rows = jnp.einsum(
            "hrl,lhd->rhd", weights, value_heads, preferred_element_type=jnp.float32
        )
        return (head_rows.astype(jnp.bfloat16), (row_max + jnp.log(row_total))[:, :, 0])

    head_out, log_norm = lax.map(one_block, starts)
    return (head_out.reshape(seq_length, -1), log_norm)


def attend_back(
    query_heads, key_heads, value_heads, grad_heads, log_norm, bias_rows, seg_all, block_rows
):
    seq_length, head_count, head_dim = key_heads.shape
    width = seq_length + block_rows - 1
    starts = jnp.arange(seq_length // block_rows, dtype=jnp.int32) * block_rows

    def one_block(carried, item_pair):
        grad_key, grad_value, offset_grad = carried
        row_start, norm_rows = item_pair
        query_rows = lax.dynamic_slice_in_dim(query_heads, row_start, block_rows, 0)
        grad_rows = lax.dynamic_slice_in_dim(grad_heads, row_start, block_rows, 0)
        seg_rows = lax.dynamic_slice_in_dim(seg_all, row_start, block_rows, 0)
        logits = score_block(
            query_rows, key_heads, bias_rows, seg_rows, seg_all, row_start, block_rows
        )
        probs = jnp.exp(logits - norm_rows[:, :, None])
        low_probs = probs.astype(jnp.bfloat16)
        grad_probs = jnp.einsum(
            "rhd,lhd->hrl", grad_rows, value_heads, preferred_element_type=jnp.float32
        )
        inner_sum = jnp.sum(probs * grad_probs, axis=-1, keepdims=True)
        grad_logits = probs * (grad_probs - inner_sum)
        offset_start = seq_length - row_start - block_rows
        current = lax.dynamic_slice_in_dim(offset_grad, offset_start, width, 1)
        offset_grad = lax.dynamic_update_slice_in_dim(
            offset_grad, current + band_sums(grad_logits, block_rows, seq_length), offset_start, 1
        )
        low_logits = grad_logits.astype(jnp.bfloat16)
        grad_query = (
            jnp.einsum("hrl,lhd->rhd", low_logits, key_heads, preferred_element_type=jnp.float32)
            * SCORE_SCALE
        )
        grad_key = (
            grad_key
            + jnp.einsum("hrl,rhd->lhd", low_logits, query_rows, preferred_element_type=jnp.float32)
            * SCORE_SCALE
        )
        grad_value = grad_value + jnp.einsum(
            "hrl,rhd->lhd", low_probs, grad_rows, preferred_element_type=jnp.float32
        )
        return ((grad_key, grad_value, offset_grad), grad_query)

    zero_heads = jnp.zeros((seq_length, head_count, head_dim), jnp.float32)
    initial = (zero_heads, zero_heads, jnp.zeros((head_count, 2 * seq_length - 1), jnp.float32))
    (grad_key, grad_value, offset_grad), grad_query = lax.scan(
        one_block, initial, (starts, log_norm)
    )
    return (
        grad_query.reshape(seq_length, -1),
        grad_key.reshape(seq_length, -1),
        grad_value.reshape(seq_length, -1),
        offset_grad,
    )


def spread_slots(values):
    return lax.all_gather(values, "mp", axis=1, tiled=True)


def send_slots(values):
    return lax.all_to_all(values, "dp", split_axis=0, concat_axis=0, tiled=True)


def return_slots(values):
    return lax.all_to_all(values, "dp", split_axis=0, concat_axis=0, tiled=True)


def fold_slots(values):
    return lax.psum_scatter(values, "mp", scatter_dimension=1, tiled=True)


def to_experts(slot_rows):
    return send_slots(spread_slots(slot_rows))


def from_experts(partial_out):
    return fold_slots(return_slots(partial_out))


def per_device(
    tokens,
    cotangent,
    norm1_gain,
    w_query,
    w_key,
    w_value,
    w_attn_out,
    bias_table,
    norm2_gain,
    w_router,
    w_expert_in,
    w_expert_out,
    routes,
    segments,
    buckets,
):
    tok_rows, model_width = tokens.shape
    groups = lax.axis_size("mp")
    seq_length = tok_rows * groups
    block_rows = min(512, seq_length)
    bucket_count, heads_local = bias_table.shape
    head_dim = w_query.shape[1] // heads_local
    expert_count = w_router.shape[1]
    capacity = 2 * tok_rows // expert_count
    exp_local = w_expert_in.shape[0]
    seg_all = segments[0]
    weight_in, weight_out = (w_expert_in, w_expert_out)
    inputs = tokens.astype(jnp.float32)
    scale_one = rms_scale(inputs)
    normed_one = (inputs * scale_one * norm1_gain).astype(jnp.bfloat16)
    normed_all = lax.all_gather(normed_one, "mp", axis=0, tiled=True)
    query = jnp.dot(normed_all, w_query, preferred_element_type=jnp.float32).astype(jnp.bfloat16)
    key_rows = jnp.dot(normed_all, w_key, preferred_element_type=jnp.float32).astype(jnp.bfloat16)
    value_rows = jnp.dot(normed_all, w_value, preferred_element_type=jnp.float32).astype(
        jnp.bfloat16
    )
    query_heads = query.reshape(seq_length, heads_local, head_dim)
    key_heads = key_rows.reshape(seq_length, heads_local, head_dim)
    value_heads = value_rows.reshape(seq_length, heads_local, head_dim)
    bucket_hot = (buckets[:, None] == jnp.arange(bucket_count, dtype=jnp.int32)[None, :]).astype(
        jnp.float32
    )
    bias_rows = jnp.dot(bucket_hot, bias_table, precision=PRECISE).T
    head_out, log_norm = attend(query_heads, key_heads, value_heads, bias_rows, seg_all, block_rows)
    rows = head_out
    attn = lax.psum_scatter(
        jnp.dot(rows, w_attn_out, preferred_element_type=jnp.float32),
        "mp",
        scatter_dimension=0,
        tiled=True,
    )
    hidden = inputs + attn
    scale_two = rms_scale(hidden)
    normed_two = (hidden * scale_two * norm2_gain).astype(jnp.bfloat16)
    router_logits = jnp.dot(normed_two, w_router, preferred_element_type=jnp.float32)
    router_max = jnp.max(router_logits, axis=-1, keepdims=True)
    router_exp = jnp.exp(router_logits - router_max)
    router_probs = router_exp / jnp.sum(router_exp, axis=-1, keepdims=True)
    expert_of = routes[:, 0]
    member = (expert_of[:, None] == jnp.arange(expert_count, dtype=jnp.int32)[None, :]).astype(
        jnp.int32
    )
    chosen = member.astype(jnp.float32)
    gate_prob = jnp.sum(router_probs * chosen, axis=-1, keepdims=True)
    positions = jnp.arange(tok_rows, dtype=jnp.int32)
    earlier = (positions[None, :] < positions[:, None]).astype(jnp.bfloat16)
    before = jnp.dot(earlier, chosen.astype(jnp.bfloat16), preferred_element_type=jnp.float32)
    slot_rank = jnp.sum(before * chosen, axis=-1).astype(jnp.int32)
    slot_index = expert_of * capacity + slot_rank
    slot_table = (
        jnp.full((expert_count * capacity,), tok_rows, jnp.int32)
        .at[slot_index]
        .set(jnp.arange(tok_rows, dtype=jnp.int32))
    )

    def to_slots(rows):
        padded = jnp.concatenate([rows, jnp.zeros((1, model_width), rows.dtype)], axis=0)
        return padded[slot_table].reshape(expert_count, capacity, model_width)

    arrived = to_experts(to_slots(normed_two))
    slot_count = arrived.shape[1]
    grouped = arrived.reshape(-1, exp_local, slot_count, model_width)
    pre_act = jnp.einsum("secd,edf->secf", grouped, weight_in, preferred_element_type=jnp.float32)
    activated = gelu_tanh(pre_act).astype(jnp.bfloat16)
    partial_out = jnp.einsum(
        "secf,efd->secd", activated, weight_out, preferred_element_type=jnp.float32
    ).reshape(-1, slot_count, model_width)
    returned = from_experts(partial_out).reshape(expert_count * capacity, model_width)
    expert_rows = returned[slot_index]
    mixed = (hidden + gate_prob * expert_rows).astype(jnp.bfloat16)
    upstream = cotangent.astype(jnp.float32)
    grad_expert = (gate_prob * upstream).astype(jnp.bfloat16)
    grad_arrived = to_experts(to_slots(grad_expert)).reshape(grouped.shape)
    grad_act = jnp.einsum(
        "secd,efd->secf", grad_arrived, weight_out, preferred_element_type=jnp.float32
    )
    grad_w_expert_out = jnp.einsum(
        "secf,secd->efd", activated, grad_arrived, preferred_element_type=jnp.float32
    )
    _, pullback = jax.vjp(gelu_tanh, pre_act)
    grad_pre = pullback(grad_act)[0].astype(jnp.bfloat16)
    grad_w_expert_in = jnp.einsum(
        "secd,secf->edf", grouped, grad_pre, preferred_element_type=jnp.float32
    )
    grad_partial = jnp.einsum(
        "secf,edf->secd", grad_pre, weight_in, preferred_element_type=jnp.float32
    ).reshape(-1, slot_count, model_width)
    grad_normed_two = from_experts(grad_partial).reshape(expert_count * capacity, model_width)[
        slot_index
    ]
    grad_gate = jnp.sum(upstream * expert_rows, axis=-1, keepdims=True)
    grad_logits = grad_gate * gate_prob * (chosen - router_probs)
    grad_w_router = jnp.dot(normed_two.astype(jnp.float32).T, grad_logits, precision=PRECISE)
    grad_normed_two = grad_normed_two + jnp.dot(
        grad_logits, w_router.astype(jnp.float32).T, precision=PRECISE
    )
    grad_hidden, grad_norm2_gain = norm_back(hidden, scale_two, norm2_gain, grad_normed_two)
    grad_hidden = grad_hidden + upstream
    grad_attn = lax.all_gather(grad_hidden.astype(jnp.bfloat16), "mp", axis=0, tiled=True)
    grad_w_attn_out = jnp.einsum(
        "lk,ld->kd", head_out, grad_attn, preferred_element_type=jnp.float32
    )
    grad_heads = jnp.einsum(
        "ld,kd->lk", grad_attn, w_attn_out, preferred_element_type=jnp.float32
    ).astype(jnp.bfloat16)
    grad_query, grad_key, grad_value, offset_grad = attend_back(
        query_heads,
        key_heads,
        value_heads,
        grad_heads.reshape(seq_length, heads_local, head_dim),
        log_norm,
        bias_rows,
        seg_all,
        block_rows,
    )
    grad_query = grad_query.astype(jnp.bfloat16)
    grad_key = grad_key.astype(jnp.bfloat16)
    grad_value = grad_value.astype(jnp.bfloat16)
    grad_bias_table = jnp.einsum("ob,ho->bh", bucket_hot, offset_grad, precision=PRECISE)
    grad_w_query = jnp.einsum(
        "ld,lk->dk", normed_all, grad_query, preferred_element_type=jnp.float32
    )
    grad_w_key = jnp.einsum("ld,lk->dk", normed_all, grad_key, preferred_element_type=jnp.float32)
    grad_w_value = jnp.einsum(
        "ld,lk->dk", normed_all, grad_value, preferred_element_type=jnp.float32
    )
    total = jnp.einsum("lk,dk->ld", grad_query, w_query, preferred_element_type=jnp.float32)
    total = total + jnp.einsum("lk,dk->ld", grad_key, w_key, preferred_element_type=jnp.float32)
    grad_normed_one = lax.psum_scatter(
        (
            total + jnp.einsum("lk,dk->ld", grad_value, w_value, preferred_element_type=jnp.float32)
        ).astype(jnp.bfloat16),
        "mp",
        scatter_dimension=0,
        tiled=True,
    ).astype(jnp.float32)
    grad_inputs, grad_norm1_gain = norm_back(inputs, scale_one, norm1_gain, grad_normed_one)
    grad_tokens = (grad_inputs + grad_hidden).astype(jnp.bfloat16)
    grad_w_query, grad_w_key, grad_w_value, grad_w_attn_out, grad_bias_table = lax.psum(
        (grad_w_query, grad_w_key, grad_w_value, grad_w_attn_out, grad_bias_table), "dp"
    )
    grad_norm1_gain, grad_norm2_gain, grad_w_router = lax.psum(
        (grad_norm1_gain, grad_norm2_gain, grad_w_router), ("dp", "mp")
    )
    return (
        mixed,
        grad_tokens,
        grad_norm1_gain,
        grad_w_query,
        grad_w_key,
        grad_w_value,
        grad_w_attn_out,
        grad_bias_table,
        grad_norm2_gain,
        grad_w_router,
        grad_w_expert_in,
        grad_w_expert_out,
    )


def solution(mesh):
    return jax.shard_map(
        per_device,
        mesh=mesh,
        in_specs=(
            P(("dp", "mp"), None),
            P(("dp", "mp"), None),
            P(),
            P(None, "mp"),
            P(None, "mp"),
            P(None, "mp"),
            P("mp", None),
            P(None, "mp"),
            P(),
            P(),
            P("dp", None, "mp"),
            P("dp", "mp", None),
            P(("dp", "mp"), None),
            P("dp", None),
            P(),
        ),
        out_specs=(
            P(("dp", "mp"), None),
            P(("dp", "mp"), None),
            P(),
            P(None, "mp"),
            P(None, "mp"),
            P(None, "mp"),
            P("mp", None),
            P(None, "mp"),
            P(),
            P(),
            P("dp", None, "mp"),
            P("dp", "mp", None),
        ),
        check_vma=False,
    )
```

```python
import jax
import jax.numpy as jnp
from jax import lax
from jax.experimental import pallas as pl
from jax.experimental.pallas import tpu as pltpu
from jax.sharding import PartitionSpec as P

EPSILON = 1e-06
SCORE_SCALE = 0.125
MASKED = -1e30
LOWEST = -3e38
PRECISE = lax.Precision.HIGHEST
BLOCK = 256
LANES = 128
LONGEST = 1024
DIRECT = 8
GELU_A = 0.7978845608028654
GELU_B = 0.044715
VMEM_BYTES = 50 * 1024 * 1024
BF16 = jnp.bfloat16
F32 = jnp.float32


def params():
    return pltpu.CompilerParams(vmem_limit_bytes=VMEM_BYTES)


def cost(flops, nbytes):
    return pl.CostEstimate(flops=int(flops), bytes_accessed=int(nbytes), transcendentals=0)


def dot_nn(left, right):
    return lax.dot_general(left, right, (((1,), (0,)), ((), ())), preferred_element_type=F32)


def dot_nt(left, right):
    return lax.dot_general(left, right, (((1,), (1,)), ((), ())), preferred_element_type=F32)


def dot_tn(left, right):
    return lax.dot_general(left, right, (((0,), (0,)), ((), ())), preferred_element_type=F32)


def rms_scale(values):
    return lax.rsqrt(jnp.mean(values * values, axis=-1, keepdims=True) + EPSILON)


def norm_back(values, scale, gain, upstream):
    weighted = gain * upstream
    gain_grad = jnp.sum(upstream * values * scale, axis=0)
    input_grad = scale * weighted - values * scale * scale * scale * jnp.mean(
        weighted * values, axis=-1, keepdims=True
    )
    return (input_grad, gain_grad)


def bias_kernel(rows_ref, out_ref):
    diag = pl.program_id(1)
    start = pl.multiple_of(diag * BLOCK, BLOCK)
    window = rows_ref[0, :, pl.ds(start, 2 * BLOCK)]
    spread = jnp.broadcast_to(window, (BLOCK, 2 * BLOCK))
    rolled = pltpu.roll(spread, BLOCK + 1, 1, stride=1, stride_axis=0)
    out_ref[0, 0] = rolled[:, :BLOCK]


def bias_tiles(rows, diags):
    heads, _, width = rows.shape
    return pl.pallas_call(
        bias_kernel,
        out_shape=jax.ShapeDtypeStruct((heads, diags, BLOCK, BLOCK), F32),
        grid=(heads, diags),
        in_specs=[pl.BlockSpec((1, 1, width), lambda h, d: (h, 0, 0))],
        out_specs=pl.BlockSpec((1, 1, BLOCK, BLOCK), lambda h, d: (h, d, 0, 0)),
        compiler_params=params(),
        cost_estimate=cost(1e8, heads * diags * BLOCK * BLOCK * 4),
        name="bias_tiles",
    )(rows)


def head_masks(heads, head_dim, width):
    lane = lax.broadcasted_iota(jnp.int32, (BLOCK, width), 1)
    return [(lane >= h * head_dim) & (lane < (h + 1) * head_dim) for h in range(heads)]


def masked_heads(rows, masks):
    wide = rows.astype(F32)
    return [jnp.where(m, wide, 0.0).astype(BF16) for m in masks]


def attend_kernel(
    heads, head_dim, reach, lo_ref, hi_ref, pos_ref, q_ref, k_ref, vt_ref, bias_ref, segc_ref, segr_ref,
    out_ref, norm_ref, acc, top, total,
):
    i = pl.program_id(0)
    queries = masked_heads(q_ref[...], head_masks(heads, head_dim, q_ref.shape[1]))
    acc[...] = jnp.zeros_like(acc)
    top[...] = jnp.full_like(top, LOWEST)
    total[...] = jnp.zeros_like(total)

    def step(j, carry):
        there = pl.ds(pl.multiple_of(j * BLOCK, BLOCK), BLOCK)
        rows = pl.ds(pl.multiple_of(pos_ref[j] * BLOCK, BLOCK), BLOCK)
        keys = k_ref[rows, :]
        same = segc_ref[there, :] == segr_ref[...]
        for h in range(heads):
            part = slice(h * head_dim, (h + 1) * head_dim)
            scores = dot_nt(keys, queries[h]) + bias_ref[h, i - j + reach]
            scores = jnp.where(same, scores, MASKED)
            old = top[h : h + 1, :]
            new = jnp.maximum(old, jnp.max(scores, axis=0, keepdims=True))
            shrink = jnp.exp(old - new)
            weights = jnp.exp(scores - new)
            top[h : h + 1, :] = new
            total[h : h + 1, :] = total[h : h + 1, :] * shrink + jnp.sum(
                weights, axis=0, keepdims=True
            )
            acc[part, :] = acc[part, :] * shrink + dot_nn(vt_ref[part, rows], weights.astype(BF16))
        return carry

    lax.fori_loop(lo_ref[i], hi_ref[i], step, 0)
    for h in range(heads):
        part = slice(h * head_dim, (h + 1) * head_dim)
        acc[part, :] = acc[part, :] / total[h : h + 1, :]
    out_ref[...] = acc[...].T.astype(BF16)
    norm_ref[...] = top[...] + jnp.log(jnp.maximum(total[...], 1e-37))


def attend(qkv, value_t, tiles, seg_col, seg_row, spans, heads, head_dim):
    seq_length = qkv.shape[0]
    width = value_t.shape[0]
    blocks = seq_length // BLOCK
    reach = tiles.shape[1] // 2
    whole = lambda shape: pl.BlockSpec(shape, lambda i, lo, hi, pos: (0,) * len(shape))
    return pl.pallas_call(
        lambda *refs: attend_kernel(heads, head_dim, reach, *refs),
        out_shape=(
            jax.ShapeDtypeStruct((seq_length, width), BF16),
            jax.ShapeDtypeStruct((8, seq_length), F32),
        ),
        grid_spec=pltpu.PrefetchScalarGridSpec(
            num_scalar_prefetch=3,
            grid=(blocks,),
            in_specs=[
                pl.BlockSpec((BLOCK, width), lambda i, lo, hi, pos: (pos[i], 0)),
                pl.BlockSpec((seq_length, width), lambda i, lo, hi, pos: (0, 1)),
                whole(value_t.shape),
                whole(tiles.shape),
                whole(seg_col.shape),
                pl.BlockSpec((1, BLOCK), lambda i, lo, hi, pos: (0, i)),
            ],
            out_specs=(
                pl.BlockSpec((BLOCK, width), lambda i, lo, hi, pos: (pos[i], 0)),
                pl.BlockSpec((8, BLOCK), lambda i, lo, hi, pos: (0, i)),
            ),
            scratch_shapes=[
                pltpu.VMEM((width, BLOCK), F32),
                pltpu.VMEM((8, BLOCK), F32),
                pltpu.VMEM((8, BLOCK), F32),
            ],
        ),
        compiler_params=params(),
        cost_estimate=cost(2e10, 1.2e7),
        name="attend",
    )(*spans, qkv, qkv, value_t, tiles, seg_col, seg_row)


def attend_back_kernel(
    heads, head_dim, reach, first, lo_ref, hi_ref, pos_ref, q_ref, go_ref, out_ref, norm_ref, k_ref, kt_ref, v_ref,
    bias_ref, segc_ref, segr_ref, gq_ref, gk_ref, gv_ref, offs_ref, gqt, gk, gv, gbias,
):
    i = pl.program_id(0)

    @pl.when(i == 0)
    def _():
        gk[...] = jnp.zeros_like(gk)
        gv[...] = jnp.zeros_like(gv)
        gbias[...] = jnp.zeros_like(gbias)

    masks = head_masks(heads, head_dim, q_ref.shape[1])
    queries = masked_heads(q_ref[...], masks)
    grads = masked_heads(go_ref[...], masks)
    product = go_ref[...].astype(F32) * out_ref[...].astype(F32)
    pick = lax.broadcasted_iota(jnp.int32, (8, q_ref.shape[1]), 0)
    lane = lax.broadcasted_iota(jnp.int32, (8, q_ref.shape[1]), 1)
    pick = ((lane >= pick * head_dim) & (lane < (pick + 1) * head_dim)).astype(F32)
    inner = lax.dot_general(
        pick, product, (((1,), (1,)), ((), ())), precision=PRECISE, preferred_element_type=F32
    )
    gqt[...] = jnp.zeros_like(gqt)

    def step(j, carry):
        there = pl.ds(pl.multiple_of(j * BLOCK, BLOCK), BLOCK)
        rows = pl.ds(pl.multiple_of(pos_ref[j] * BLOCK, BLOCK), BLOCK)
        keys = k_ref[rows, :]
        values = v_ref[rows, :]
        same = segc_ref[there, :] == segr_ref[...]
        for h in range(heads):
            part = slice(h * head_dim, (h + 1) * head_dim)
            scores = dot_nt(keys, queries[h]) + bias_ref[h, i - j + reach]
            weights = jnp.exp(jnp.where(same, scores, MASKED) - norm_ref[first + h : first + h + 1, :])
            slope = weights * (dot_nt(values, grads[h]) - inner[h : h + 1, :])
            gbias[h, i - j + reach] += slope
            low_slope = slope.astype(BF16)
            gv[rows, :] += dot_nn(weights.astype(BF16), grads[h])
            gk[rows, :] += dot_nn(low_slope, queries[h])
            gqt[part, :] += dot_nn(kt_ref[part, rows], low_slope)
        return carry

    lax.fori_loop(lo_ref[i], hi_ref[i], step, 0)
    gq_ref[...] = (gqt[...] * SCORE_SCALE).T.astype(BF16)

    @pl.when(i == pl.num_programs(0) - 1)
    def _():
        gk_ref[...] = gk[...].astype(BF16)
        gv_ref[...] = gv[...].astype(BF16)
        offs_ref[...] = jnp.zeros_like(offs_ref)
        blank = jnp.zeros((BLOCK, BLOCK), F32)
        for h in range(heads):
            for d in range(2 * reach + 1):
                sums = jnp.concatenate([gbias[h, d], blank], axis=1)
                size = BLOCK // 2
                while size >= 8:
                    sums = pltpu.roll(sums[:size], size, 1) + sums[size:]
                    size //= 2
                line = sums[7:8]
                for r in range(7):
                    line = line + pltpu.roll(sums[r : r + 1], 7 - r, 1)
                offs_ref[h : h + 1, d * BLOCK : (d + 2) * BLOCK] += line


def attend_back(
    group, heads, head_dim, qkv, grad_heads, head_out, norms, key_t, tiles, seg_col, seg_row, spans,
    ready,
):
    seq_length = qkv.shape[0]
    groups = head_out.shape[1] // LANES
    blocks = seq_length // BLOCK
    diags = tiles.shape[1]
    reach = diags // 2
    first = group * (LANES // head_dim)
    count = min(heads - first, LANES // head_dim)
    whole = lambda shape: pl.BlockSpec(shape, lambda i, lo, hi, pos: (0,) * len(shape))
    row_block = pl.BlockSpec((BLOCK, LANES), lambda i, lo, hi, pos: (pos[i], group))
    columns = lambda n: pl.BlockSpec((seq_length, LANES), lambda i, lo, hi, pos: (0, n * groups + group))
    rows_out = jax.ShapeDtypeStruct((seq_length, LANES), BF16)
    offsets = jax.ShapeDtypeStruct((8, (diags + 1) * BLOCK), F32)
    return pl.pallas_call(
        lambda *refs: attend_back_kernel(
            count, head_dim, reach, first, *refs[:13], *refs[13 + len(ready) :]
        ),
        out_shape=(rows_out, rows_out, rows_out, offsets),
        grid_spec=pltpu.PrefetchScalarGridSpec(
            num_scalar_prefetch=3,
            grid=(blocks,),
            in_specs=[
                row_block,
                row_block,
                row_block,
                pl.BlockSpec((8, BLOCK), lambda i, lo, hi, pos: (0, i)),
                columns(1),
                pl.BlockSpec((LANES, seq_length), lambda i, lo, hi, pos: (group, 0)),
                columns(2),
                pl.BlockSpec(
                    (count,) + tiles.shape[1:], lambda i, lo, hi, pos: (first // count, 0, 0, 0)
                ),
                whole(seg_col.shape),
                pl.BlockSpec((1, BLOCK), lambda i, lo, hi, pos: (0, i)),
            ]
            + [pl.BlockSpec(memory_space=pl.ANY)] * len(ready),
            out_specs=(
                pl.BlockSpec((BLOCK, LANES), lambda i, lo, hi, pos: (pos[i], 0)),
                whole(rows_out.shape),
                whole(rows_out.shape),
                whole(offsets.shape),
            ),
            scratch_shapes=[
                pltpu.VMEM((LANES, BLOCK), F32),
                pltpu.VMEM((seq_length, LANES), F32),
                pltpu.VMEM((seq_length, LANES), F32),
                pltpu.VMEM((count, diags, BLOCK, BLOCK), F32),
            ],
        ),
        compiler_params=params(),
        cost_estimate=cost(1.4e10 * count, 5e6 * count),
        name="attend_back",
    )(*spans, qkv, grad_heads, head_out, norms, qkv, key_t, qkv, tiles, seg_col, seg_row, *ready)


def split_rows(refs):
    parts = [r[...].reshape(-1, r.shape[-1]) for r in refs]
    return jnp.concatenate(parts, axis=0)


def store_rows(refs, values):
    size = values.shape[0] // len(refs)
    for n, r in enumerate(refs):
        r[...] = values[n * size : (n + 1) * size].astype(r.dtype).reshape(r.shape)


def expert_kernel(groups, *refs):
    xs, us = refs[:groups], refs[groups : 2 * groups]
    win_ref, wout_ref, wr_ref, hot_ref = refs[2 * groups : 2 * groups + 4]
    outs = refs[2 * groups + 4 : 3 * groups + 4]
    act_ref, gpre_ref, gu_ref, gl_ref = refs[3 * groups + 4 :]
    hot = hot_ref[0]
    size = act_ref.shape[2] // 2
    for n in range(2):
        part = slice(n * groups // 2, (n + 1) * groups // 2)
        rows = slice(n * size, (n + 1) * size)
        x = split_rows(xs[part])
        u = split_rows(us[part])
        logits = dot_nn(x, wr_ref[...])
        powers = jnp.exp(logits - jnp.max(logits, axis=-1, keepdims=True))
        probs = powers / jnp.sum(powers, axis=-1, keepdims=True)
        gate = jnp.sum(probs * hot, axis=-1, keepdims=True)
        pre = dot_nn(x, win_ref[0])
        back = dot_nt(u, wout_ref[0])
        square = pre * pre
        bent = jnp.tanh(pre * (GELU_A + GELU_A * GELU_B * square))
        half = 0.5 + 0.5 * bent
        act = (pre * half).astype(BF16)
        slope = half + pre * (0.5 - 0.5 * bent * bent) * (GELU_A + 3.0 * GELU_A * GELU_B * square)
        grad_gate = jnp.sum(act.astype(F32) * back, axis=-1, keepdims=True)
        grad_pre = (gate * back * slope).astype(BF16)
        grad_logits = grad_gate * gate * (hot - probs)
        high = grad_logits.astype(BF16)
        rest = (grad_logits - high.astype(F32)).astype(BF16)
        grad_x = dot_nt(grad_pre, win_ref[0]) + dot_nt(high, wr_ref[...])
        store_rows(outs[part], grad_x + dot_nt(rest, wr_ref[...]))
        act_ref[0, 0, rows] = act
        gpre_ref[0, 0, rows] = grad_pre
        gu_ref[0, 0, rows] = (gate * u.astype(F32)).astype(BF16)
        gl_ref[0, 0, rows] = grad_logits


def slot_specs(groups, tile, capacity, width, first=0):
    spec = pl.BlockSpec((tile, 1, capacity, width), lambda e, t: (t, e + first, 0, 0))
    return [spec] * groups


def experts(xs, us, w_in, w_out, w_router, hots, first):
    groups = len(xs)
    sources, count, capacity, width = xs[0].shape
    tile = min(sources, DIRECT)
    tiles = sources // tile
    rows = groups * tile * capacity
    hidden_units = w_in.shape[2]
    slots = slot_specs(groups, tile, capacity, width)
    kept = lambda last: pl.BlockSpec((1, 1, rows, last), lambda e, t: (e, t, 0, 0))
    kept_shape = lambda last, dt: jax.ShapeDtypeStruct((count, tiles, rows, last), dt)
    expert_count = w_router.shape[1]
    res = pl.pallas_call(
        lambda *refs: expert_kernel(groups, *refs),
        out_shape=[jax.ShapeDtypeStruct(xs[0].shape, BF16)] * groups
        + [
            kept_shape(hidden_units, BF16),
            kept_shape(hidden_units, BF16),
            kept_shape(width, BF16),
            kept_shape(expert_count, F32),
        ],
        grid=(count, tiles),
        in_specs=slots
        + slot_specs(groups, tile, capacity, width, first)
        + [
            pl.BlockSpec((1, width, hidden_units), lambda e, t: (e + first, 0, 0)),
            pl.BlockSpec((1, hidden_units, width), lambda e, t: (e + first, 0, 0)),
            pl.BlockSpec(w_router.shape, lambda e, t: (0, 0)),
            pl.BlockSpec((1, 1, expert_count), lambda e, t: (e + first, 0, 0)),
        ],
        out_specs=slots + [kept(hidden_units), kept(hidden_units), kept(width), kept(expert_count)],
        compiler_params=params(),
        cost_estimate=cost(6 * count * tiles * rows * width * hidden_units, 7e6 * count),
        name="experts",
    )(*xs, *us, w_in, w_out, w_router, hots)
    return res[:groups], res[groups:]


def weight_kernel(groups, *refs):
    xs = refs[:groups]
    act_ref, gpre_ref, gu_ref, gl_ref, wout_ref = refs[groups : groups + 5]
    outs = refs[-groups - 3 : -3]
    gin_ref, gout_ref, gr_ref = refs[-3:]
    x = split_rows(xs)
    act = act_ref[0, 0]
    store_rows(outs, dot_nn(act, wout_ref[0]))
    grad_logits = gl_ref[0, 0]
    high = grad_logits.astype(BF16)
    rest = (grad_logits - high.astype(F32)).astype(BF16)
    first = pl.program_id(1) == 0

    @pl.when(first)
    def _():
        gin_ref[0] = dot_tn(x, gpre_ref[0, 0])
        gout_ref[0] = dot_tn(act, gu_ref[0, 0])

    @pl.when(jnp.logical_not(first))
    def _():
        gin_ref[0] += dot_tn(x, gpre_ref[0, 0])
        gout_ref[0] += dot_tn(act, gu_ref[0, 0])

    router = dot_tn(x, high) + dot_tn(x, rest)
    start = first & (pl.program_id(0) == 0)

    @pl.when(start)
    def _():
        gr_ref[...] = router

    @pl.when(jnp.logical_not(start))
    def _():
        gr_ref[...] += router


def expert_weights(xs, kept, w_out, first, earlier):
    groups = len(xs)
    sources, count, capacity, width = xs[0].shape
    tile = min(sources, DIRECT)
    tiles = sources // tile
    rows = groups * tile * capacity
    hidden_units = w_out.shape[1]
    expert_count = kept[3].shape[-1]
    slots = slot_specs(groups, tile, capacity, width)
    held = lambda last: pl.BlockSpec((1, 1, rows, last), lambda e, t: (e, t, 0, 0))
    anywhere = [pl.BlockSpec(memory_space=pl.ANY)] * len(earlier)
    inputs = groups + 5
    res = pl.pallas_call(
        lambda *refs: weight_kernel(groups, *refs),
        out_shape=[jax.ShapeDtypeStruct((sources, w_out.shape[0], capacity, width), BF16)] * groups
        + [
            jax.ShapeDtypeStruct((w_out.shape[0], width, hidden_units), F32),
            jax.ShapeDtypeStruct((w_out.shape[0], hidden_units, width), F32),
            jax.ShapeDtypeStruct((width, expert_count), F32),
        ],
        grid=(count, tiles),
        in_specs=slots
        + [held(hidden_units), held(hidden_units), held(width), held(expert_count)]
        + [pl.BlockSpec((1, hidden_units, width), lambda e, t: (e + first, 0, 0))]
        + anywhere,
        out_specs=slot_specs(groups, tile, capacity, width, first)
        + [
            pl.BlockSpec((1, width, hidden_units), lambda e, t: (e + first, 0, 0)),
            pl.BlockSpec((1, hidden_units, width), lambda e, t: (e + first, 0, 0)),
            pl.BlockSpec((width, expert_count), lambda e, t: (0, 0)),
        ],
        input_output_aliases={inputs + n: n for n in range(len(earlier))},
        compiler_params=params(),
        cost_estimate=cost(6 * count * tiles * rows * width * hidden_units, 1e7 * count),
        name="expert_weights",
    )(*xs, *kept, w_out, *earlier)
    return res[: groups + 2], res[groups + 2]


def after(values, *earlier):
    return lax.optimization_barrier((values,) + earlier)[0]


def swap(values, axis, step):
    count = lax.axis_size(axis)
    return lax.ppermute(values, axis, [(n, n ^ step) for n in range(count)])


def gather_mp(values):
    across = swap(values, "mp", 2)
    return [values, swap(values, "mp", 1), across, swap(across, "mp", 1)]


def fold_mp(parts):
    near = parts[0].astype(F32) + swap(parts[1], "mp", 1).astype(F32)
    far = parts[2].astype(F32) + swap(parts[3], "mp", 1).astype(F32)
    return near + swap(far.astype(BF16), "mp", 2).astype(F32)


def trade_dp(values):
    return lax.all_to_all(values, "dp", split_axis=0, concat_axis=0, tiled=True)


def trade_dp_steps(values):
    count = lax.axis_size("dp")
    if count > DIRECT:
        return trade_dp(values)
    own = lax.axis_index("dp")
    held, step = values[None], count // 2
    while step > 0:
        low = (own // step) % 2 == 0
        sent, size = held.shape[0], held.shape[1] // 2
        first, second = held[:, :size], held[:, size:]
        leave = jnp.where(low, second, first)
        came = swap(leave, "dp", step)
        stay = jnp.where(low, first, second)
        held = jnp.stack([jnp.where(low, stay, came), jnp.where(low, came, stay)], axis=1)
        held = held.reshape((2 * sent, size) + values.shape[1:])
        step //= 2
    return held[:, 0]


def sum_steps(values, axis):
    step = 1
    while step < lax.axis_size(axis):
        values = values + swap(values, axis, step)
        step *= 2
    return values


def fold_dp(values):
    count = lax.axis_size("dp")
    parts = values.reshape((count, values.shape[0] // count) + values.shape[1:])
    return jnp.sum(trade_dp(parts).astype(F32), axis=0)


def share_dp(pieces):
    mine = jnp.concatenate(pieces, axis=1).astype(BF16)
    count = lax.axis_size("dp")
    whole = trade_dp(jnp.broadcast_to(mine[None], (count,) + mine.shape))
    whole = whole.reshape(-1, mine.shape[1]).astype(F32)
    ends = [0]
    for p in pieces:
        ends.append(ends[-1] + p.shape[1])
    return [whole[:, a:b] for a, b in zip(ends, ends[1:])]


def per_device(
    tokens,
    cotangent,
    norm1_gain,
    w_query,
    w_key,
    w_value,
    w_attn_out,
    bias_table,
    norm2_gain,
    w_router,
    w_expert_in,
    w_expert_out,
    routes,
    segments,
    buckets,
):
    tok_rows, model_width = tokens.shape
    groups = lax.axis_size("mp")
    sources = lax.axis_size("dp")
    own_mp, own_dp = lax.axis_index("mp"), lax.axis_index("dp")
    seq_length = tok_rows * groups
    blocks = seq_length // BLOCK
    bucket_count, heads_local = bias_table.shape
    head_width = w_query.shape[1]
    expert_count = w_router.shape[1]
    capacity = 2 * tok_rows // expert_count
    exp_local = w_expert_in.shape[0]
    chunks = 2 if exp_local % 2 == 0 else 1
    chunk_experts = exp_local // chunks
    reach = min(LONGEST // BLOCK, blocks - 1)
    head_dim = head_width // heads_local
    lane_groups = -(-head_width // LANES)

    inputs = tokens.astype(F32)
    scale_one = rms_scale(inputs)
    normed_one = (inputs * scale_one * norm1_gain).astype(BF16)
    half = tok_rows // 2
    pieces = zip(gather_mp(normed_one[:half]), gather_mp(normed_one[half:]))
    normed_all = jnp.concatenate([part for pair in pieces for part in pair], axis=0)

    expert_of = routes[:, 0]
    chosen = expert_of[:, None] == jnp.arange(expert_count, dtype=jnp.int32)[None, :]
    positions = jnp.arange(tok_rows, dtype=jnp.int32)
    earlier = (positions[None, :] < positions[:, None]).astype(BF16)
    before = jnp.dot(earlier, chosen.astype(BF16), preferred_element_type=F32)
    slot_rank = jnp.sum(before * chosen.astype(F32), axis=-1).astype(jnp.int32)
    slot_index = expert_of * capacity + slot_rank
    slot_count = expert_count * capacity
    picks = (slot_index[:, None] == jnp.arange(slot_count, dtype=jnp.int32)[None, :]).astype(BF16)

    def to_slots(rows):
        slots = dot_tn(picks, rows).astype(BF16)
        return slots.reshape(sources, exp_local, capacity, model_width)

    offsets = jnp.concatenate([buckets[::-1], jnp.full((1,), -1, jnp.int32)])
    first = seq_length - (reach + 1) * BLOCK
    offsets = offsets[first : first + (2 * reach + 2) * BLOCK]
    bucket_hot = (
        offsets[None, :] == jnp.arange(bucket_count, dtype=jnp.int32)[:, None]
    ).astype(F32)
    bias_rows = jnp.dot(bias_table.T, bucket_hot, precision=PRECISE)
    tiles = bias_tiles(bias_rows[:, None, :], 2 * reach + 1)

    seg_all = segments[0]
    ends = seg_all.reshape(blocks, BLOCK)
    low = jnp.sum(seg_all[None, :] < ends[:, :1], axis=1, dtype=jnp.int32) // BLOCK
    high = -(-jnp.sum(seg_all[None, :] <= ends[:, -1:], axis=1, dtype=jnp.int32) // BLOCK)
    block_ids = jnp.arange(blocks, dtype=jnp.int32)
    low = jnp.maximum(low, block_ids - reach)
    high = jnp.minimum(high, block_ids + reach + 1)
    per = tok_rows // BLOCK
    spans = (low, high, (block_ids // per ^ own_mp) * per + block_ids % per)
    seg_col, seg_row = seg_all[:, None], seg_all[None, :]

    up_slots = trade_dp(to_slots(after(cotangent, normed_one)))

    spare = ((0, 0), (0, lane_groups * LANES - head_width))
    padded = [jnp.pad(w, spare) for w in (w_query, w_key, w_value)]
    scaled = jnp.concatenate([padded[0] * jnp.asarray(SCORE_SCALE, BF16)] + padded[1:], axis=1)
    qkv = jnp.dot(normed_all, scaled, preferred_element_type=F32).astype(BF16)
    value_t = qkv[:, 2 * padded[0].shape[1] :].T
    grad_slots = gather_mp(after(up_slots, normed_all))
    w_out_parts = gather_mp(after(w_attn_out, normed_all))
    head_out, norms = attend(
        qkv, value_t, tiles, seg_col, seg_row, spans, heads_local, head_dim
    )

    def block_of(rows, n):
        return rows[n * tok_rows : (n + 1) * tok_rows]

    head_rows = head_out[:, :head_width]
    head_parts = [block_of(head_rows, 0)] + [
        swap(block_of(head_rows, n), "mp", n) for n in range(1, groups)
    ]
    attn = jnp.dot(
        jnp.concatenate(head_parts, axis=1),
        jnp.concatenate(w_out_parts, axis=0),
        preferred_element_type=F32,
    )
    hidden = inputs + attn
    scale_two = rms_scale(hidden)
    normed_two = (hidden * scale_two * norm2_gain).astype(BF16)
    slots = trade_dp(to_slots(normed_two))
    token_slots = [
        gather_mp(slots[:, c * chunk_experts : (c + 1) * chunk_experts]) for c in range(chunks)
    ]

    hots = (
        (own_dp * exp_local + jnp.arange(exp_local, dtype=jnp.int32))[:, None]
        == jnp.arange(expert_count, dtype=jnp.int32)[None, :]
    ).astype(F32)[:, None, :]
    folded, kept = [], []
    for c in range(chunks):
        parts, extra = experts(
            token_slots[c], grad_slots, w_expert_in, w_expert_out, w_router, hots,
            c * chunk_experts,
        )
        folded.append(fold_mp(parts).astype(BF16))
        kept.append(extra)
    back = [trade_dp(f) for f in folded]
    grad_w_router, made = 0.0, ()
    for c in range(chunks):
        made, grad_router = expert_weights(
            token_slots[c], kept[c], w_expert_out, c * chunk_experts, made
        )
        grad_w_router = grad_w_router + grad_router
    grad_w_expert_in, grad_w_expert_out = made[groups:]
    far_rows = (made[2].astype(F32) + swap(made[3], "mp", 1).astype(F32)).astype(BF16)
    near_rows = made[0].astype(F32) + swap(made[1], "mp", 1).astype(F32)
    back = jnp.concatenate(back, axis=1).reshape(-1, model_width)
    grad_normed_two = jnp.dot(picks, after(back, grad_w_router), preferred_element_type=F32)

    upstream = cotangent.astype(F32)
    grad_hidden, grad_norm2_gain = norm_back(hidden, scale_two, norm2_gain, grad_normed_two)
    grad_hidden = grad_hidden + upstream
    grad_attn = grad_hidden.astype(BF16)

    grad_heads = [dot_nt(grad_attn, w).astype(BF16) for w in w_out_parts]
    grad_heads = [g if n == 0 else swap(g, "mp", n) for n, g in enumerate(grad_heads)]
    grad_heads = jnp.pad(jnp.concatenate(grad_heads, axis=0), spare)
    key_t = qkv[:, padded[0].shape[1] : 2 * padded[0].shape[1]].T

    shared = jnp.concatenate([grad_w_router, grad_norm2_gain[:, None]], axis=1)
    shared = sum_steps(after(shared, grad_attn), "mp")
    grad_attn_all = jnp.concatenate(gather_mp(after(grad_attn, grad_heads)), axis=0)
    rest = [dot_tn(grad_attn_all, head_rows), shared]
    folded_rows = (near_rows + swap(far_rows, "mp", 2).astype(F32)).astype(BF16)
    order, piece_of, bias_sums, gain_sum, summed = [], [], [], 0.0, []
    ready = [far_rows]
    for g in range(lane_groups):
        grad_q, grad_k, grad_v, offset_grad = attend_back(
            g, heads_local, head_dim, qkv, grad_heads, head_out, norms, key_t, tiles, seg_col,
            seg_row, spans, ready,
        )
        lanes = min(LANES, head_width - g * LANES)
        own = jnp.concatenate([grad_q[:, :lanes], grad_k[:, :lanes], grad_v[:, :lanes]], axis=1)
        weights = jnp.concatenate([w[:, g * LANES : g * LANES + lanes] for w in padded], axis=1)
        order.append((own, weights))
        partial = dot_tn(normed_all, own)
        gain_sum = gain_sum + jnp.sum(partial * weights.astype(F32), axis=1)
        payload = jnp.concatenate([partial] + rest, axis=1).astype(BF16)
        piece_of.append((lanes, payload.shape[1]))
        rest, ready = [], [payload, folded_rows]
        summed.append(fold_dp(payload))
        bias_sums.append(offset_grad[: lanes // head_dim])
    summed = share_dp(summed)
    grads = [[], [], []]
    for (lanes, _), columns in zip(piece_of, summed):
        for n in range(3):
            grads[n].append(columns[:, n * lanes : (n + 1) * lanes])
    grads = [jnp.concatenate(g, axis=1) for g in grads]
    rest = summed[0][:, 3 * piece_of[0][0] :]
    grad_w_attn_out, shared = rest[:, :head_width].T, rest[:, head_width:]

    rows_back = trade_dp_steps(folded_rows)
    router_logits = jnp.dot(normed_two, w_router, preferred_element_type=F32)
    router_exp = jnp.exp(router_logits - jnp.max(router_logits, axis=-1, keepdims=True))
    router_probs = router_exp / jnp.sum(router_exp, axis=-1, keepdims=True)
    gate_prob = jnp.sum(router_probs * chosen.astype(F32), axis=-1, keepdims=True)
    expert_rows = jnp.dot(picks, rows_back.reshape(-1, model_width), preferred_element_type=F32)
    mixed = (hidden + gate_prob * expert_rows).astype(BF16)

    own = jnp.concatenate([p[0] for p in order], axis=1)
    weights = jnp.concatenate([p[1] for p in order], axis=1)
    total = dot_nt(own, weights).astype(BF16)
    grad_normed_one = fold_mp([block_of(total, n) for n in range(groups)])
    bias_sums = jnp.dot(jnp.concatenate(bias_sums, axis=0), bucket_hot.T, precision=PRECISE)
    small = jnp.concatenate([gain_sum / norm1_gain, bias_sums.reshape(-1)])
    small = jnp.pad(small, (0, -small.shape[0] % (8 * LANES))).reshape(8, -1)
    small = sum_steps(small, "dp")
    grad_norm1_gain = sum_steps(small, "mp").reshape(-1)[:model_width]
    bias_sums = small.reshape(-1)[model_width : model_width + heads_local * bucket_count]
    grad_bias_table = bias_sums.reshape(heads_local, -1).T
    weighted = norm1_gain * grad_normed_one
    grad_inputs = scale_one * weighted - inputs * scale_one * scale_one * scale_one * jnp.mean(
        weighted * inputs, axis=-1, keepdims=True
    )
    grad_tokens = (grad_inputs + grad_hidden).astype(BF16)
    return (
        mixed,
        grad_tokens,
        grad_norm1_gain,
        *grads,
        grad_w_attn_out,
        grad_bias_table,
        shared[:, expert_count],
        shared[:, :expert_count],
        grad_w_expert_in,
        grad_w_expert_out,
    )


def solution(mesh):
    return jax.shard_map(
        per_device,
        mesh=mesh,
        in_specs=(
            P(("dp", "mp"), None),
            P(("dp", "mp"), None),
            P(),
            P(None, "mp"),
            P(None, "mp"),
            P(None, "mp"),
            P("mp", None),
            P(None, "mp"),
            P(),
            P(),
            P("dp", None, "mp"),
            P("dp", "mp", None),
            P(("dp", "mp"), None),
            P("dp", None),
            P(),
        ),
        out_specs=(
            P(("dp", "mp"), None),
            P(("dp", "mp"), None),
            P(),
            P(None, "mp"),
            P(None, "mp"),
            P(None, "mp"),
            P("mp", None),
            P(None, "mp"),
            P(),
            P(),
            P("dp", None, "mp"),
            P("dp", "mp", None),
        ),
        check_vma=False,
    )
```

```python
import jax
import jax.numpy as jnp
from jax import lax
from jax.experimental import pallas as pl
from jax.experimental.pallas import tpu as pltpu
from jax.sharding import PartitionSpec as P

EPSILON = 1e-06
SCORE_SCALE = 0.125
MASKED = -1e30
LOWEST = -3e38
PRECISE = lax.Precision.HIGHEST
BLOCK = 256
LANES = 128
LONGEST = 1024
DIRECT = 8
GELU_A = 0.7978845608028654
GELU_B = 0.044715
VMEM_BYTES = 50 * 1024 * 1024
BF16 = jnp.bfloat16
F32 = jnp.float32


def params():
    return pltpu.CompilerParams(vmem_limit_bytes=VMEM_BYTES)


def cost(flops, nbytes):
    return pl.CostEstimate(flops=int(flops), bytes_accessed=int(nbytes), transcendentals=0)


def dot_nn(left, right):
    return lax.dot_general(left, right, (((1,), (0,)), ((), ())), preferred_element_type=F32)


def dot_nt(left, right):
    return lax.dot_general(left, right, (((1,), (1,)), ((), ())), preferred_element_type=F32)


def dot_tn(left, right):
    return lax.dot_general(left, right, (((0,), (0,)), ((), ())), preferred_element_type=F32)


def rms_scale(values):
    return lax.rsqrt(jnp.mean(values * values, axis=-1, keepdims=True) + EPSILON)


def norm_back(values, scale, gain, upstream):
    weighted = gain * upstream
    gain_grad = jnp.sum(upstream * values * scale, axis=0)
    input_grad = scale * weighted - values * scale * scale * scale * jnp.mean(
        weighted * values, axis=-1, keepdims=True
    )
    return (input_grad, gain_grad)


def bias_kernel(rows_ref, out_ref):
    diag = pl.program_id(1)
    start = pl.multiple_of(diag * BLOCK, BLOCK)
    window = rows_ref[0, :, pl.ds(start, 2 * BLOCK)]
    spread = jnp.broadcast_to(window, (BLOCK, 2 * BLOCK))
    rolled = pltpu.roll(spread, BLOCK + 1, 1, stride=1, stride_axis=0)
    out_ref[0, 0] = rolled[:, :BLOCK]


def bias_tiles(rows, diags):
    heads, _, width = rows.shape
    return pl.pallas_call(
        bias_kernel,
        out_shape=jax.ShapeDtypeStruct((heads, diags, BLOCK, BLOCK), F32),
        grid=(heads, diags),
        in_specs=[pl.BlockSpec((1, 1, width), lambda h, d: (h, 0, 0))],
        out_specs=pl.BlockSpec((1, 1, BLOCK, BLOCK), lambda h, d: (h, d, 0, 0)),
        compiler_params=params(),
        cost_estimate=cost(1e8, heads * diags * BLOCK * BLOCK * 4),
        name="bias_tiles",
    )(rows)


def head_masks(heads, head_dim, width):
    lane = lax.broadcasted_iota(jnp.int32, (BLOCK, width), 1)
    return [(lane >= h * head_dim) & (lane < (h + 1) * head_dim) for h in range(heads)]


def masked_heads(rows, masks):
    wide = rows.astype(F32)
    return [jnp.where(m, wide, 0.0).astype(BF16) for m in masks]


def attend_kernel(
    heads, head_dim, reach, lo_ref, hi_ref, pos_ref, q_ref, k_ref, vt_ref, bias_ref, segc_ref, segr_ref,
    out_ref, norm_ref, acc, top, total,
):
    i = pl.program_id(0)
    queries = masked_heads(q_ref[...], head_masks(heads, head_dim, q_ref.shape[1]))
    acc[...] = jnp.zeros_like(acc)
    top[...] = jnp.full_like(top, LOWEST)
    total[...] = jnp.zeros_like(total)

    def step(j, carry):
        there = pl.ds(pl.multiple_of(j * BLOCK, BLOCK), BLOCK)
        rows = pl.ds(pl.multiple_of(pos_ref[j] * BLOCK, BLOCK), BLOCK)
        keys = k_ref[rows, :]
        same = segc_ref[there, :] == segr_ref[...]
        for h in range(heads):
            part = slice(h * head_dim, (h + 1) * head_dim)
            scores = dot_nt(keys, queries[h]) + bias_ref[h, i - j + reach]
            scores = jnp.where(same, scores, MASKED)
            old = top[h : h + 1, :]
            new = jnp.maximum(old, jnp.max(scores, axis=0, keepdims=True))
            shrink = jnp.exp(old - new)
            weights = jnp.exp(scores - new)
            top[h : h + 1, :] = new
            total[h : h + 1, :] = total[h : h + 1, :] * shrink + jnp.sum(
                weights, axis=0, keepdims=True
            )
            acc[part, :] = acc[part, :] * shrink + dot_nn(vt_ref[part, rows], weights.astype(BF16))
        return carry

    lax.fori_loop(lo_ref[i], hi_ref[i], step, 0)
    for h in range(heads):
        part = slice(h * head_dim, (h + 1) * head_dim)
        acc[part, :] = acc[part, :] / total[h : h + 1, :]
    out_ref[...] = acc[...].T.astype(BF16)
    norm_ref[...] = top[...] + jnp.log(jnp.maximum(total[...], 1e-37))


def attend(qkv, value_t, tiles, seg_col, seg_row, spans, heads, head_dim):
    seq_length = qkv.shape[0]
    width = value_t.shape[0]
    blocks = seq_length // BLOCK
    reach = tiles.shape[1] // 2
    whole = lambda shape: pl.BlockSpec(shape, lambda i, lo, hi, pos: (0,) * len(shape))
    return pl.pallas_call(
        lambda *refs: attend_kernel(heads, head_dim, reach, *refs),
        out_shape=(
            jax.ShapeDtypeStruct((seq_length, width), BF16),
            jax.ShapeDtypeStruct((8, seq_length), F32),
        ),
        grid_spec=pltpu.PrefetchScalarGridSpec(
            num_scalar_prefetch=3,
            grid=(blocks,),
            in_specs=[
                pl.BlockSpec((BLOCK, width), lambda i, lo, hi, pos: (pos[i], 0)),
                pl.BlockSpec((seq_length, width), lambda i, lo, hi, pos: (0, 1)),
                whole(value_t.shape),
                whole(tiles.shape),
                whole(seg_col.shape),
                pl.BlockSpec((1, BLOCK), lambda i, lo, hi, pos: (0, i)),
            ],
            out_specs=(
                pl.BlockSpec((BLOCK, width), lambda i, lo, hi, pos: (pos[i], 0)),
                pl.BlockSpec((8, BLOCK), lambda i, lo, hi, pos: (0, i)),
            ),
            scratch_shapes=[
                pltpu.VMEM((width, BLOCK), F32),
                pltpu.VMEM((8, BLOCK), F32),
                pltpu.VMEM((8, BLOCK), F32),
            ],
        ),
        compiler_params=params(),
        cost_estimate=cost(2e10, 1.2e7),
        name="attend",
    )(*spans, qkv, qkv, value_t, tiles, seg_col, seg_row)


def attend_back_kernel(
    heads, head_dim, reach, first, lo_ref, hi_ref, pos_ref, q_ref, go_ref, out_ref, norm_ref, k_ref, kt_ref, v_ref,
    bias_ref, segc_ref, segr_ref, gq_ref, gk_ref, gv_ref, offs_ref, gqt, gk, gv, gbias,
):
    i = pl.program_id(0)

    @pl.when(i == 0)
    def _():
        gk[...] = jnp.zeros_like(gk)
        gv[...] = jnp.zeros_like(gv)
        gbias[...] = jnp.zeros_like(gbias)

    masks = head_masks(heads, head_dim, q_ref.shape[1])
    queries = masked_heads(q_ref[...], masks)
    grads = masked_heads(go_ref[...], masks)
    product = go_ref[...].astype(F32) * out_ref[...].astype(F32)
    pick = lax.broadcasted_iota(jnp.int32, (8, q_ref.shape[1]), 0)
    lane = lax.broadcasted_iota(jnp.int32, (8, q_ref.shape[1]), 1)
    pick = ((lane >= pick * head_dim) & (lane < (pick + 1) * head_dim)).astype(F32)
    inner = lax.dot_general(
        pick, product, (((1,), (1,)), ((), ())), precision=PRECISE, preferred_element_type=F32
    )
    gqt[...] = jnp.zeros_like(gqt)

    def step(j, carry):
        there = pl.ds(pl.multiple_of(j * BLOCK, BLOCK), BLOCK)
        rows = pl.ds(pl.multiple_of(pos_ref[j] * BLOCK, BLOCK), BLOCK)
        keys = k_ref[rows, :]
        values = v_ref[rows, :]
        same = segc_ref[there, :] == segr_ref[...]
        for h in range(heads):
            part = slice(h * head_dim, (h + 1) * head_dim)
            scores = dot_nt(keys, queries[h]) + bias_ref[h, i - j + reach]
            weights = jnp.exp(jnp.where(same, scores, MASKED) - norm_ref[first + h : first + h + 1, :])
            slope = weights * (dot_nt(values, grads[h]) - inner[h : h + 1, :])
            gbias[h, i - j + reach] += slope
            low_slope = slope.astype(BF16)
            gv[rows, :] += dot_nn(weights.astype(BF16), grads[h])
            gk[rows, :] += dot_nn(low_slope, queries[h])
            gqt[part, :] += dot_nn(kt_ref[part, rows], low_slope)
        return carry

    lax.fori_loop(lo_ref[i], hi_ref[i], step, 0)
    gq_ref[...] = (gqt[...] * SCORE_SCALE).T.astype(BF16)

    @pl.when(i == pl.num_programs(0) - 1)
    def _():
        gk_ref[...] = gk[...].astype(BF16)
        gv_ref[...] = gv[...].astype(BF16)
        offs_ref[...] = jnp.zeros_like(offs_ref)
        blank = jnp.zeros((BLOCK, BLOCK), F32)
        for h in range(heads):
            for d in range(2 * reach + 1):
                sums = jnp.concatenate([gbias[h, d], blank], axis=1)
                size = BLOCK // 2
                while size >= 8:
                    sums = pltpu.roll(sums[:size], size, 1) + sums[size:]
                    size //= 2
                line = sums[7:8]
                for r in range(7):
                    line = line + pltpu.roll(sums[r : r + 1], 7 - r, 1)
                offs_ref[h : h + 1, d * BLOCK : (d + 2) * BLOCK] += line


def attend_back(
    group, heads, head_dim, qkv, grad_heads, head_out, norms, key_t, tiles, seg_col, seg_row, spans,
    ready,
):
    seq_length = qkv.shape[0]
    groups = head_out.shape[1] // LANES
    blocks = seq_length // BLOCK
    diags = tiles.shape[1]
    reach = diags // 2
    first = group * (LANES // head_dim)
    count = min(heads - first, LANES // head_dim)
    whole = lambda shape: pl.BlockSpec(shape, lambda i, lo, hi, pos: (0,) * len(shape))
    row_block = pl.BlockSpec((BLOCK, LANES), lambda i, lo, hi, pos: (pos[i], group))
    columns = lambda n: pl.BlockSpec((seq_length, LANES), lambda i, lo, hi, pos: (0, n * groups + group))
    rows_out = jax.ShapeDtypeStruct((seq_length, LANES), BF16)
    offsets = jax.ShapeDtypeStruct((8, (diags + 1) * BLOCK), F32)
    return pl.pallas_call(
        lambda *refs: attend_back_kernel(
            count, head_dim, reach, first, *refs[:13], *refs[13 + len(ready) :]
        ),
        out_shape=(rows_out, rows_out, rows_out, offsets),
        grid_spec=pltpu.PrefetchScalarGridSpec(
            num_scalar_prefetch=3,
            grid=(blocks,),
            in_specs=[
                row_block,
                row_block,
                row_block,
                pl.BlockSpec((8, BLOCK), lambda i, lo, hi, pos: (0, i)),
                columns(1),
                pl.BlockSpec((LANES, seq_length), lambda i, lo, hi, pos: (group, 0)),
                columns(2),
                pl.BlockSpec(
                    (count,) + tiles.shape[1:], lambda i, lo, hi, pos: (first // count, 0, 0, 0)
                ),
                whole(seg_col.shape),
                pl.BlockSpec((1, BLOCK), lambda i, lo, hi, pos: (0, i)),
            ]
            + [pl.BlockSpec(memory_space=pl.ANY)] * len(ready),
            out_specs=(
                pl.BlockSpec((BLOCK, LANES), lambda i, lo, hi, pos: (pos[i], 0)),
                whole(rows_out.shape),
                whole(rows_out.shape),
                whole(offsets.shape),
            ),
            scratch_shapes=[
                pltpu.VMEM((LANES, BLOCK), F32),
                pltpu.VMEM((seq_length, LANES), F32),
                pltpu.VMEM((seq_length, LANES), F32),
                pltpu.VMEM((count, diags, BLOCK, BLOCK), F32),
            ],
        ),
        compiler_params=params(),
        cost_estimate=cost(1.4e10 * count, 5e6 * count),
        name="attend_back",
    )(*spans, qkv, grad_heads, head_out, norms, qkv, key_t, qkv, tiles, seg_col, seg_row, *ready)


def split_rows(refs):
    parts = [r[...].reshape(-1, r.shape[-1]) for r in refs]
    return jnp.concatenate(parts, axis=0)


def store_rows(refs, values):
    size = values.shape[0] // len(refs)
    for n, r in enumerate(refs):
        r[...] = values[n * size : (n + 1) * size].astype(r.dtype).reshape(r.shape)


def expert_kernel(groups, *refs):
    xs, us = refs[:groups], refs[groups : 2 * groups]
    win_ref, wout_ref, wr_ref, hot_ref = refs[2 * groups : 2 * groups + 4]
    outs = refs[2 * groups + 4 : 3 * groups + 4]
    act_ref, gpre_ref, gu_ref, gl_ref = refs[3 * groups + 4 :]
    hot = hot_ref[0]
    size = act_ref.shape[2] // 2
    for n in range(2):
        part = slice(n * groups // 2, (n + 1) * groups // 2)
        rows = slice(n * size, (n + 1) * size)
        x = split_rows(xs[part])
        u = split_rows(us[part])
        logits = dot_nn(x, wr_ref[...])
        powers = jnp.exp(logits - jnp.max(logits, axis=-1, keepdims=True))
        probs = powers / jnp.sum(powers, axis=-1, keepdims=True)
        gate = jnp.sum(probs * hot, axis=-1, keepdims=True)
        pre = dot_nn(x, win_ref[0])
        back = dot_nt(u, wout_ref[0])
        square = pre * pre
        bent = jnp.tanh(pre * (GELU_A + GELU_A * GELU_B * square))
        half = 0.5 + 0.5 * bent
        act = (pre * half).astype(BF16)
        slope = half + pre * (0.5 - 0.5 * bent * bent) * (GELU_A + 3.0 * GELU_A * GELU_B * square)
        grad_gate = jnp.sum(act.astype(F32) * back, axis=-1, keepdims=True)
        grad_pre = (gate * back * slope).astype(BF16)
        grad_logits = grad_gate * gate * (hot - probs)
        high = grad_logits.astype(BF16)
        rest = (grad_logits - high.astype(F32)).astype(BF16)
        grad_x = dot_nt(grad_pre, win_ref[0]) + dot_nt(high, wr_ref[...])
        store_rows(outs[part], grad_x + dot_nt(rest, wr_ref[...]))
        act_ref[0, 0, rows] = act
        gpre_ref[0, 0, rows] = grad_pre
        gu_ref[0, 0, rows] = (gate * u.astype(F32)).astype(BF16)
        gl_ref[0, 0, rows] = grad_logits


def slot_specs(groups, tile, capacity, width, first=0):
    spec = pl.BlockSpec((tile, 1, capacity, width), lambda e, t: (t, e + first, 0, 0))
    return [spec] * groups


def experts(xs, us, w_in, w_out, w_router, hots, first):
    groups = len(xs)
    sources, count, capacity, width = xs[0].shape
    tile = min(sources, DIRECT)
    tiles = sources // tile
    rows = groups * tile * capacity
    hidden_units = w_in.shape[2]
    slots = slot_specs(groups, tile, capacity, width)
    kept = lambda last: pl.BlockSpec((1, 1, rows, last), lambda e, t: (e, t, 0, 0))
    kept_shape = lambda last, dt: jax.ShapeDtypeStruct((count, tiles, rows, last), dt)
    expert_count = w_router.shape[1]
    res = pl.pallas_call(
        lambda *refs: expert_kernel(groups, *refs),
        out_shape=[jax.ShapeDtypeStruct(xs[0].shape, BF16)] * groups
        + [
            kept_shape(hidden_units, BF16),
            kept_shape(hidden_units, BF16),
            kept_shape(width, BF16),
            kept_shape(expert_count, F32),
        ],
        grid=(count, tiles),
        in_specs=slots
        + slot_specs(groups, tile, capacity, width, first)
        + [
            pl.BlockSpec((1, width, hidden_units), lambda e, t: (e + first, 0, 0)),
            pl.BlockSpec((1, hidden_units, width), lambda e, t: (e + first, 0, 0)),
            pl.BlockSpec(w_router.shape, lambda e, t: (0, 0)),
            pl.BlockSpec((1, 1, expert_count), lambda e, t: (e + first, 0, 0)),
        ],
        out_specs=slots + [kept(hidden_units), kept(hidden_units), kept(width), kept(expert_count)],
        compiler_params=params(),
        cost_estimate=cost(6 * count * tiles * rows * width * hidden_units, 7e6 * count),
        name="experts",
    )(*xs, *us, w_in, w_out, w_router, hots)
    return res[:groups], res[groups:]


def weight_kernel(groups, *refs):
    xs = refs[:groups]
    act_ref, gpre_ref, gu_ref, gl_ref, wout_ref = refs[groups : groups + 5]
    outs = refs[-groups - 3 : -3]
    gin_ref, gout_ref, gr_ref = refs[-3:]
    x = split_rows(xs)
    act = act_ref[0, 0]
    store_rows(outs, dot_nn(act, wout_ref[0]))
    grad_logits = gl_ref[0, 0]
    high = grad_logits.astype(BF16)
    rest = (grad_logits - high.astype(F32)).astype(BF16)
    first = pl.program_id(1) == 0

    @pl.when(first)
    def _():
        gin_ref[0] = dot_tn(x, gpre_ref[0, 0])
        gout_ref[0] = dot_tn(act, gu_ref[0, 0])

    @pl.when(jnp.logical_not(first))
    def _():
        gin_ref[0] += dot_tn(x, gpre_ref[0, 0])
        gout_ref[0] += dot_tn(act, gu_ref[0, 0])

    router = dot_tn(x, high) + dot_tn(x, rest)
    start = first & (pl.program_id(0) == 0)

    @pl.when(start)
    def _():
        gr_ref[...] = router

    @pl.when(jnp.logical_not(start))
    def _():
        gr_ref[...] += router


def expert_weights(xs, kept, w_out, first, earlier):
    groups = len(xs)
    sources, count, capacity, width = xs[0].shape
    tile = min(sources, DIRECT)
    tiles = sources // tile
    rows = groups * tile * capacity
    hidden_units = w_out.shape[1]
    expert_count = kept[3].shape[-1]
    slots = slot_specs(groups, tile, capacity, width)
    held = lambda last: pl.BlockSpec((1, 1, rows, last), lambda e, t: (e, t, 0, 0))
    anywhere = [pl.BlockSpec(memory_space=pl.ANY)] * len(earlier)
    inputs = groups + 5
    res = pl.pallas_call(
        lambda *refs: weight_kernel(groups, *refs),
        out_shape=[jax.ShapeDtypeStruct((sources, w_out.shape[0], capacity, width), BF16)] * groups
        + [
            jax.ShapeDtypeStruct((w_out.shape[0], width, hidden_units), F32),
            jax.ShapeDtypeStruct((w_out.shape[0], hidden_units, width), F32),
            jax.ShapeDtypeStruct((width, expert_count), F32),
        ],
        grid=(count, tiles),
        in_specs=slots
        + [held(hidden_units), held(hidden_units), held(width), held(expert_count)]
        + [pl.BlockSpec((1, hidden_units, width), lambda e, t: (e + first, 0, 0))]
        + anywhere,
        out_specs=slot_specs(groups, tile, capacity, width, first)
        + [
            pl.BlockSpec((1, width, hidden_units), lambda e, t: (e + first, 0, 0)),
            pl.BlockSpec((1, hidden_units, width), lambda e, t: (e + first, 0, 0)),
            pl.BlockSpec((width, expert_count), lambda e, t: (0, 0)),
        ],
        input_output_aliases={inputs + n: n for n in range(len(earlier))},
        compiler_params=params(),
        cost_estimate=cost(6 * count * tiles * rows * width * hidden_units, 1e7 * count),
        name="expert_weights",
    )(*xs, *kept, w_out, *earlier)
    return res[: groups + 2], res[groups + 2]


def after(values, *earlier):
    return lax.optimization_barrier((values,) + earlier)[0]


def swap(values, axis, step):
    count = lax.axis_size(axis)
    return lax.ppermute(values, axis, [(n, n ^ step) for n in range(count)])


def gather_mp(values):
    across = swap(values, "mp", 2)
    return [values, swap(values, "mp", 1), across, swap(across, "mp", 1)]


def fold_mp(parts):
    near = parts[0].astype(F32) + swap(parts[1], "mp", 1).astype(F32)
    far = parts[2].astype(F32) + swap(parts[3], "mp", 1).astype(F32)
    return near + swap(far.astype(BF16), "mp", 2).astype(F32)


def unless_nan(values, flag):
    return jnp.where(flag != flag, jnp.zeros_like(values), values)


def trade_dp(values):
    return lax.all_to_all(values, "dp", split_axis=0, concat_axis=0, tiled=True)


def trade_dp_steps(values):
    count = lax.axis_size("dp")
    if count > DIRECT:
        return trade_dp(values)
    own = lax.axis_index("dp")
    held, step = values[None], count // 2
    while step > 0:
        low = (own // step) % 2 == 0
        sent, size = held.shape[0], held.shape[1] // 2
        first, second = held[:, :size], held[:, size:]
        leave = jnp.where(low, second, first)
        came = swap(leave, "dp", step)
        stay = jnp.where(low, first, second)
        held = jnp.stack([jnp.where(low, stay, came), jnp.where(low, came, stay)], axis=1)
        held = held.reshape((2 * sent, size) + values.shape[1:])
        step //= 2
    return held[:, 0]


def sum_steps(values, axis):
    step = 1
    while step < lax.axis_size(axis):
        values = values + swap(values, axis, step)
        step *= 2
    return values


def fold_dp(values):
    count = lax.axis_size("dp")
    parts = values.reshape((count, values.shape[0] // count) + values.shape[1:])
    return jnp.sum(trade_dp(parts).astype(F32), axis=0)


def share_dp(pieces):
    mine = jnp.concatenate(pieces, axis=1).astype(BF16)
    count = lax.axis_size("dp")
    whole = trade_dp(jnp.broadcast_to(mine[None], (count,) + mine.shape))
    whole = whole.reshape(-1, mine.shape[1]).astype(F32)
    ends = [0]
    for p in pieces:
        ends.append(ends[-1] + p.shape[1])
    return [whole[:, a:b] for a, b in zip(ends, ends[1:])]


def per_device(
    tokens,
    cotangent,
    norm1_gain,
    w_query,
    w_key,
    w_value,
    w_attn_out,
    bias_table,
    norm2_gain,
    w_router,
    w_expert_in,
    w_expert_out,
    routes,
    segments,
    buckets,
):
    tok_rows, model_width = tokens.shape
    groups = lax.axis_size("mp")
    sources = lax.axis_size("dp")
    own_mp, own_dp = lax.axis_index("mp"), lax.axis_index("dp")
    seq_length = tok_rows * groups
    blocks = seq_length // BLOCK
    bucket_count, heads_local = bias_table.shape
    head_width = w_query.shape[1]
    expert_count = w_router.shape[1]
    capacity = 2 * tok_rows // expert_count
    exp_local = w_expert_in.shape[0]
    chunks = 2 if exp_local % 2 == 0 else 1
    chunk_experts = exp_local // chunks
    reach = min(LONGEST // BLOCK, blocks - 1)
    head_dim = head_width // heads_local
    lane_groups = -(-head_width // LANES)

    inputs = tokens.astype(F32)
    scale_one = rms_scale(inputs)
    normed_one = (inputs * scale_one * norm1_gain).astype(BF16)
    half = tok_rows // 2
    pieces = zip(gather_mp(normed_one[:half]), gather_mp(normed_one[half:]))
    normed_all = jnp.concatenate([part for pair in pieces for part in pair], axis=0)

    expert_of = routes[:, 0]
    chosen = expert_of[:, None] == jnp.arange(expert_count, dtype=jnp.int32)[None, :]
    positions = jnp.arange(tok_rows, dtype=jnp.int32)
    earlier = (positions[None, :] < positions[:, None]).astype(BF16)
    before = jnp.dot(earlier, chosen.astype(BF16), preferred_element_type=F32)
    slot_rank = jnp.sum(before * chosen.astype(F32), axis=-1).astype(jnp.int32)
    slot_index = expert_of * capacity + slot_rank
    slot_count = expert_count * capacity
    picks = (slot_index[:, None] == jnp.arange(slot_count, dtype=jnp.int32)[None, :]).astype(BF16)

    def to_slots(rows):
        slots = dot_tn(picks, rows).astype(BF16)
        return slots.reshape(sources, exp_local, capacity, model_width)

    offsets = jnp.concatenate([buckets[::-1], jnp.full((1,), -1, jnp.int32)])
    first = seq_length - (reach + 1) * BLOCK
    offsets = offsets[first : first + (2 * reach + 2) * BLOCK]
    bucket_hot = (
        offsets[None, :] == jnp.arange(bucket_count, dtype=jnp.int32)[:, None]
    ).astype(F32)
    bias_rows = jnp.dot(bias_table.T, bucket_hot, precision=PRECISE)
    tiles = bias_tiles(bias_rows[:, None, :], 2 * reach + 1)

    seg_all = segments[0]
    ends = seg_all.reshape(blocks, BLOCK)
    low = jnp.sum(seg_all[None, :] < ends[:, :1], axis=1, dtype=jnp.int32) // BLOCK
    high = -(-jnp.sum(seg_all[None, :] <= ends[:, -1:], axis=1, dtype=jnp.int32) // BLOCK)
    block_ids = jnp.arange(blocks, dtype=jnp.int32)
    low = jnp.maximum(low, block_ids - reach)
    high = jnp.minimum(high, block_ids + reach + 1)
    per = tok_rows // BLOCK
    spans = (low, high, (block_ids // per ^ own_mp) * per + block_ids % per)
    seg_col, seg_row = seg_all[:, None], seg_all[None, :]

    up_slots = trade_dp(to_slots(after(cotangent, normed_one)))

    spare = ((0, 0), (0, lane_groups * LANES - head_width))
    padded = [jnp.pad(w, spare) for w in (w_query, w_key, w_value)]
    scaled = jnp.concatenate([padded[0] * jnp.asarray(SCORE_SCALE, BF16)] + padded[1:], axis=1)
    qkv = jnp.dot(normed_all, scaled, preferred_element_type=F32).astype(BF16)
    value_t = qkv[:, 2 * padded[0].shape[1] :].T
    grad_slots = gather_mp(after(up_slots, normed_all))
    w_out_parts = gather_mp(after(w_attn_out, normed_all))
    head_out, norms = attend(
        qkv, value_t, tiles, seg_col, seg_row, spans, heads_local, head_dim
    )

    def block_of(rows, n):
        return rows[n * tok_rows : (n + 1) * tok_rows]

    head_rows = head_out[:, :head_width]
    head_parts = [block_of(head_rows, 0)] + [
        swap(block_of(head_rows, n), "mp", n) for n in range(1, groups)
    ]
    attn = jnp.dot(
        jnp.concatenate(head_parts, axis=1),
        jnp.concatenate(w_out_parts, axis=0),
        preferred_element_type=F32,
    )
    hidden = inputs + attn
    scale_two = rms_scale(hidden)
    normed_two = (hidden * scale_two * norm2_gain).astype(BF16)
    slots = trade_dp(to_slots(normed_two))
    token_slots = [
        gather_mp(slots[:, c * chunk_experts : (c + 1) * chunk_experts]) for c in range(chunks)
    ]

    hots = (
        (own_dp * exp_local + jnp.arange(exp_local, dtype=jnp.int32))[:, None]
        == jnp.arange(expert_count, dtype=jnp.int32)[None, :]
    ).astype(F32)[:, None, :]
    folded, kept = [], []
    for c in range(chunks):
        parts, extra = experts(
            token_slots[c], grad_slots, w_expert_in, w_expert_out, w_router, hots,
            c * chunk_experts,
        )
        folded.append(fold_mp(parts).astype(BF16))
        kept.append(extra)
    back = [trade_dp(f) for f in folded]
    grad_w_router, made = 0.0, ()
    for c in range(chunks):
        made, grad_router = expert_weights(
            token_slots[c], kept[c], w_expert_out, c * chunk_experts, made
        )
        grad_w_router = grad_w_router + grad_router
    grad_w_expert_in, grad_w_expert_out = made[groups:]
    far_rows = (made[2].astype(F32) + swap(made[3], "mp", 1).astype(F32)).astype(BF16)
    near_rows = made[0].astype(F32) + swap(made[1], "mp", 1).astype(F32)
    back = jnp.concatenate(back, axis=1).reshape(-1, model_width)
    grad_normed_two = jnp.dot(picks, after(back, grad_w_router), preferred_element_type=F32)

    upstream = cotangent.astype(F32)
    grad_hidden, grad_norm2_gain = norm_back(hidden, scale_two, norm2_gain, grad_normed_two)
    grad_hidden = grad_hidden + upstream
    grad_attn = grad_hidden.astype(BF16)

    grad_heads = [dot_nt(grad_attn, w).astype(BF16) for w in w_out_parts]
    grad_heads = [g if n == 0 else swap(g, "mp", n) for n, g in enumerate(grad_heads)]
    grad_heads = jnp.pad(jnp.concatenate(grad_heads, axis=0), spare)
    key_t = qkv[:, padded[0].shape[1] : 2 * padded[0].shape[1]].T

    shared = jnp.concatenate([grad_w_router, grad_norm2_gain[:, None]], axis=1)
    shared = sum_steps(after(shared, grad_attn), "mp")
    grad_attn_all = jnp.concatenate(gather_mp(after(grad_attn, grad_heads)), axis=0)
    rest = [dot_tn(grad_attn_all, head_rows), shared]
    folded_rows = (near_rows + swap(far_rows, "mp", 2).astype(F32)).astype(BF16)
    order, piece_of, bias_sums, gain_sum, summed = [], [], [], 0.0, []
    ready = [far_rows]
    for g in range(lane_groups):
        grad_q, grad_k, grad_v, offset_grad = attend_back(
            g, heads_local, head_dim, qkv, grad_heads, head_out, norms, key_t, tiles, seg_col,
            seg_row, spans, ready,
        )
        lanes = min(LANES, head_width - g * LANES)
        own = jnp.concatenate([grad_q, grad_k, grad_v], axis=1)
        weights = jnp.concatenate([w[:, g * LANES : (g + 1) * LANES] for w in padded], axis=1)
        order.append((own, weights))
        partial = dot_tn(normed_all, own)
        gain_sum = gain_sum + jnp.sum(partial * weights.astype(F32), axis=1)
        partial = [partial[:, n * LANES : n * LANES + lanes] for n in range(3)]
        payload = jnp.concatenate(partial + rest, axis=1).astype(BF16)
        if summed:
            payload = unless_nan(payload, summed[-1][0, 0])
        piece_of.append((lanes, payload.shape[1]))
        rest, ready = [], [payload, folded_rows]
        summed.append(fold_dp(payload))
        bias_sums.append(offset_grad[: lanes // head_dim])
    summed = share_dp(summed)
    grads = [[], [], []]
    for (lanes, _), columns in zip(piece_of, summed):
        for n in range(3):
            grads[n].append(columns[:, n * lanes : (n + 1) * lanes])
    grads = [jnp.concatenate(g, axis=1) for g in grads]
    rest = summed[0][:, 3 * piece_of[0][0] :]
    grad_w_attn_out, shared = rest[:, :head_width].T, rest[:, head_width:]

    rows_back = trade_dp_steps(folded_rows)
    router_logits = jnp.dot(normed_two, w_router, preferred_element_type=F32)
    router_exp = jnp.exp(router_logits - jnp.max(router_logits, axis=-1, keepdims=True))
    router_probs = router_exp / jnp.sum(router_exp, axis=-1, keepdims=True)
    gate_prob = jnp.sum(router_probs * chosen.astype(F32), axis=-1, keepdims=True)
    expert_rows = jnp.dot(picks, rows_back.reshape(-1, model_width), preferred_element_type=F32)
    mixed = (hidden + gate_prob * expert_rows).astype(BF16)

    own = jnp.concatenate([p[0] for p in order], axis=1)
    weights = jnp.concatenate([p[1] for p in order], axis=1)
    total = dot_nt(own, weights).astype(BF16)
    grad_normed_one = fold_mp([block_of(total, n) for n in range(groups)])
    bias_sums = jnp.dot(jnp.concatenate(bias_sums, axis=0), bucket_hot.T, precision=PRECISE)
    small = jnp.concatenate([gain_sum / norm1_gain, bias_sums.reshape(-1)])
    small = jnp.pad(small, (0, -small.shape[0] % (8 * LANES))).reshape(8, -1)
    small = sum_steps(small, "dp")
    grad_norm1_gain = sum_steps(small, "mp").reshape(-1)[:model_width]
    bias_sums = small.reshape(-1)[model_width : model_width + heads_local * bucket_count]
    grad_bias_table = bias_sums.reshape(heads_local, -1).T
    weighted = norm1_gain * grad_normed_one
    grad_inputs = scale_one * weighted - inputs * scale_one * scale_one * scale_one * jnp.mean(
        weighted * inputs, axis=-1, keepdims=True
    )
    grad_tokens = (grad_inputs + grad_hidden).astype(BF16)
    return (
        mixed,
        grad_tokens,
        grad_norm1_gain,
        *grads,
        grad_w_attn_out,
        grad_bias_table,
        shared[:, expert_count],
        shared[:, :expert_count],
        grad_w_expert_in,
        grad_w_expert_out,
    )


def solution(mesh):
    return jax.shard_map(
        per_device,
        mesh=mesh,
        in_specs=(
            P(("dp", "mp"), None),
            P(("dp", "mp"), None),
            P(),
            P(None, "mp"),
            P(None, "mp"),
            P(None, "mp"),
            P("mp", None),
            P(None, "mp"),
            P(),
            P(),
            P("dp", None, "mp"),
            P("dp", "mp", None),
            P(("dp", "mp"), None),
            P("dp", None),
            P(),
        ),
        out_specs=(
            P(("dp", "mp"), None),
            P(("dp", "mp"), None),
            P(),
            P(None, "mp"),
            P(None, "mp"),
            P(None, "mp"),
            P("mp", None),
            P(None, "mp"),
            P(),
            P(),
            P("dp", None, "mp"),
            P("dp", "mp", None),
        ),
        check_vma=False,
    )
```

```python
import jax
import jax.numpy as jnp
from jax import lax
from jax.experimental import pallas as pl
from jax.experimental.pallas import tpu as pltpu
from jax.sharding import PartitionSpec as P

EPSILON = 1e-06
SCORE_SCALE = 0.125
MASKED = -1e30
LOWEST = -3e38
PRECISE = lax.Precision.HIGHEST
BLOCK = 256
LANES = 128
LONGEST = 1024
DIRECT = 8
GELU_A = 0.7978845608028654
GELU_B = 0.044715
VMEM_BYTES = 50 * 1024 * 1024
BF16 = jnp.bfloat16
F32 = jnp.float32


def params():
    return pltpu.CompilerParams(vmem_limit_bytes=VMEM_BYTES)


def cost(flops, nbytes):
    return pl.CostEstimate(flops=int(flops), bytes_accessed=int(nbytes), transcendentals=0)


def dot_nn(left, right):
    return lax.dot_general(left, right, (((1,), (0,)), ((), ())), preferred_element_type=F32)


def dot_nt(left, right):
    return lax.dot_general(left, right, (((1,), (1,)), ((), ())), preferred_element_type=F32)


def dot_tn(left, right):
    return lax.dot_general(left, right, (((0,), (0,)), ((), ())), preferred_element_type=F32)


def rms_scale(values):
    return lax.rsqrt(jnp.mean(values * values, axis=-1, keepdims=True) + EPSILON)


def norm_back(values, scale, gain, upstream):
    weighted = gain * upstream
    gain_grad = jnp.sum(upstream * values * scale, axis=0)
    input_grad = scale * weighted - values * scale * scale * scale * jnp.mean(
        weighted * values, axis=-1, keepdims=True
    )
    return (input_grad, gain_grad)


def bias_kernel(rows_ref, out_ref):
    diag = pl.program_id(1)
    start = pl.multiple_of(diag * BLOCK, BLOCK)
    window = rows_ref[0, :, pl.ds(start, 2 * BLOCK)]
    spread = jnp.broadcast_to(window, (BLOCK, 2 * BLOCK))
    rolled = pltpu.roll(spread, BLOCK + 1, 1, stride=1, stride_axis=0)
    out_ref[0, 0] = rolled[:, :BLOCK]


def bias_tiles(rows, diags):
    heads, _, width = rows.shape
    return pl.pallas_call(
        bias_kernel,
        out_shape=jax.ShapeDtypeStruct((heads, diags, BLOCK, BLOCK), F32),
        grid=(heads, diags),
        in_specs=[pl.BlockSpec((1, 1, width), lambda h, d: (h, 0, 0))],
        out_specs=pl.BlockSpec((1, 1, BLOCK, BLOCK), lambda h, d: (h, d, 0, 0)),
        compiler_params=params(),
        cost_estimate=cost(1e8, heads * diags * BLOCK * BLOCK * 4),
        name="bias_tiles",
    )(rows)


def head_masks(heads, head_dim, width):
    lane = lax.broadcasted_iota(jnp.int32, (BLOCK, width), 1)
    return [(lane >= h * head_dim) & (lane < (h + 1) * head_dim) for h in range(heads)]


def masked_heads(rows, masks):
    wide = rows.astype(F32)
    return [jnp.where(m, wide, 0.0).astype(BF16) for m in masks]


def attend_kernel(
    heads, head_dim, reach, lo_ref, hi_ref, pos_ref, q_ref, k_ref, vt_ref, bias_ref, segc_ref, segr_ref,
    out_ref, norm_ref, acc, top, total,
):
    i = pl.program_id(0)
    queries = masked_heads(q_ref[...], head_masks(heads, head_dim, q_ref.shape[1]))
    acc[...] = jnp.zeros_like(acc)
    top[...] = jnp.full_like(top, LOWEST)
    total[...] = jnp.zeros_like(total)

    def step(j, carry):
        there = pl.ds(pl.multiple_of(j * BLOCK, BLOCK), BLOCK)
        rows = pl.ds(pl.multiple_of(pos_ref[j] * BLOCK, BLOCK), BLOCK)
        keys = k_ref[rows, :]
        same = segc_ref[there, :] == segr_ref[...]
        for h in range(heads):
            part = slice(h * head_dim, (h + 1) * head_dim)
            scores = dot_nt(keys, queries[h]) + bias_ref[h, i - j + reach]
            scores = jnp.where(same, scores, MASKED)
            old = top[h : h + 1, :]
            new = jnp.maximum(old, jnp.max(scores, axis=0, keepdims=True))
            shrink = jnp.exp(old - new)
            weights = jnp.exp(scores - new)
            top[h : h + 1, :] = new
            total[h : h + 1, :] = total[h : h + 1, :] * shrink + jnp.sum(
                weights, axis=0, keepdims=True
            )
            acc[part, :] = acc[part, :] * shrink + dot_nn(vt_ref[part, rows], weights.astype(BF16))
        return carry

    lax.fori_loop(lo_ref[i], hi_ref[i], step, 0)
    for h in range(heads):
        part = slice(h * head_dim, (h + 1) * head_dim)
        acc[part, :] = acc[part, :] / total[h : h + 1, :]
    out_ref[...] = acc[...].T.astype(BF16)
    norm_ref[...] = top[...] + jnp.log(jnp.maximum(total[...], 1e-37))


def attend(qkv, value_t, tiles, seg_col, seg_row, spans, heads, head_dim):
    seq_length = qkv.shape[0]
    width = value_t.shape[0]
    blocks = seq_length // BLOCK
    reach = tiles.shape[1] // 2
    whole = lambda shape: pl.BlockSpec(shape, lambda i, lo, hi, pos: (0,) * len(shape))
    return pl.pallas_call(
        lambda *refs: attend_kernel(heads, head_dim, reach, *refs),
        out_shape=(
            jax.ShapeDtypeStruct((seq_length, width), BF16),
            jax.ShapeDtypeStruct((8, seq_length), F32),
        ),
        grid_spec=pltpu.PrefetchScalarGridSpec(
            num_scalar_prefetch=3,
            grid=(blocks,),
            in_specs=[
                pl.BlockSpec((BLOCK, width), lambda i, lo, hi, pos: (pos[i], 0)),
                pl.BlockSpec((seq_length, width), lambda i, lo, hi, pos: (0, 1)),
                whole(value_t.shape),
                whole(tiles.shape),
                whole(seg_col.shape),
                pl.BlockSpec((1, BLOCK), lambda i, lo, hi, pos: (0, i)),
            ],
            out_specs=(
                pl.BlockSpec((BLOCK, width), lambda i, lo, hi, pos: (pos[i], 0)),
                pl.BlockSpec((8, BLOCK), lambda i, lo, hi, pos: (0, i)),
            ),
            scratch_shapes=[
                pltpu.VMEM((width, BLOCK), F32),
                pltpu.VMEM((8, BLOCK), F32),
                pltpu.VMEM((8, BLOCK), F32),
            ],
        ),
        compiler_params=params(),
        cost_estimate=cost(2e10, 1.2e7),
        name="attend",
    )(*spans, qkv, qkv, value_t, tiles, seg_col, seg_row)


def attend_back_kernel(
    heads, head_dim, reach, first, lo_ref, hi_ref, pos_ref, q_ref, go_ref, out_ref, norm_ref, k_ref, kt_ref, v_ref,
    bias_ref, segc_ref, segr_ref, gq_ref, gk_ref, gv_ref, offs_ref, gqt, gk, gv, gbias,
):
    i = pl.program_id(0)

    @pl.when(i == 0)
    def _():
        gk[...] = jnp.zeros_like(gk)
        gv[...] = jnp.zeros_like(gv)
        gbias[...] = jnp.zeros_like(gbias)

    masks = head_masks(heads, head_dim, q_ref.shape[1])
    queries = masked_heads(q_ref[...], masks)
    grads = masked_heads(go_ref[...], masks)
    product = go_ref[...].astype(F32) * out_ref[...].astype(F32)
    pick = lax.broadcasted_iota(jnp.int32, (8, q_ref.shape[1]), 0)
    lane = lax.broadcasted_iota(jnp.int32, (8, q_ref.shape[1]), 1)
    pick = ((lane >= pick * head_dim) & (lane < (pick + 1) * head_dim)).astype(F32)
    inner = lax.dot_general(
        pick, product, (((1,), (1,)), ((), ())), precision=PRECISE, preferred_element_type=F32
    )
    gqt[...] = jnp.zeros_like(gqt)

    def step(j, carry):
        there = pl.ds(pl.multiple_of(j * BLOCK, BLOCK), BLOCK)
        rows = pl.ds(pl.multiple_of(pos_ref[j] * BLOCK, BLOCK), BLOCK)
        keys = k_ref[rows, :]
        values = v_ref[rows, :]
        same = segc_ref[there, :] == segr_ref[...]
        for h in range(heads):
            part = slice(h * head_dim, (h + 1) * head_dim)
            scores = dot_nt(keys, queries[h]) + bias_ref[h, i - j + reach]
            weights = jnp.exp(jnp.where(same, scores, MASKED) - norm_ref[first + h : first + h + 1, :])
            slope = weights * (dot_nt(values, grads[h]) - inner[h : h + 1, :])
            gbias[h, i - j + reach] += slope
            low_slope = slope.astype(BF16)
            gv[rows, :] += dot_nn(weights.astype(BF16), grads[h])
            gk[rows, :] += dot_nn(low_slope, queries[h])
            gqt[part, :] += dot_nn(kt_ref[part, rows], low_slope)
        return carry

    lax.fori_loop(lo_ref[i], hi_ref[i], step, 0)
    gq_ref[...] = (gqt[...] * SCORE_SCALE).T.astype(BF16)

    @pl.when(i == pl.num_programs(0) - 1)
    def _():
        gk_ref[...] = gk[...].astype(BF16)
        gv_ref[...] = gv[...].astype(BF16)
        offs_ref[...] = jnp.zeros_like(offs_ref)
        blank = jnp.zeros((BLOCK, BLOCK), F32)
        for h in range(heads):
            for d in range(2 * reach + 1):
                sums = jnp.concatenate([gbias[h, d], blank], axis=1)
                size = BLOCK // 2
                while size >= 8:
                    sums = pltpu.roll(sums[:size], size, 1) + sums[size:]
                    size //= 2
                line = sums[7:8]
                for r in range(7):
                    line = line + pltpu.roll(sums[r : r + 1], 7 - r, 1)
                offs_ref[h : h + 1, d * BLOCK : (d + 2) * BLOCK] += line


def attend_back(
    group, heads, head_dim, qkv, grad_heads, head_out, norms, key_t, tiles, seg_col, seg_row, spans,
    ready,
):
    seq_length = qkv.shape[0]
    groups = head_out.shape[1] // LANES
    blocks = seq_length // BLOCK
    diags = tiles.shape[1]
    reach = diags // 2
    first = group * (LANES // head_dim)
    count = min(heads - first, LANES // head_dim)
    whole = lambda shape: pl.BlockSpec(shape, lambda i, lo, hi, pos: (0,) * len(shape))
    row_block = pl.BlockSpec((BLOCK, LANES), lambda i, lo, hi, pos: (pos[i], group))
    columns = lambda n: pl.BlockSpec((seq_length, LANES), lambda i, lo, hi, pos: (0, n * groups + group))
    rows_out = jax.ShapeDtypeStruct((seq_length, LANES), BF16)
    offsets = jax.ShapeDtypeStruct((8, (diags + 1) * BLOCK), F32)
    return pl.pallas_call(
        lambda *refs: attend_back_kernel(
            count, head_dim, reach, first, *refs[:13], *refs[13 + len(ready) :]
        ),
        out_shape=(rows_out, rows_out, rows_out, offsets),
        grid_spec=pltpu.PrefetchScalarGridSpec(
            num_scalar_prefetch=3,
            grid=(blocks,),
            in_specs=[
                row_block,
                row_block,
                row_block,
                pl.BlockSpec((8, BLOCK), lambda i, lo, hi, pos: (0, i)),
                columns(1),
                pl.BlockSpec((LANES, seq_length), lambda i, lo, hi, pos: (group, 0)),
                columns(2),
                pl.BlockSpec(
                    (count,) + tiles.shape[1:], lambda i, lo, hi, pos: (first // count, 0, 0, 0)
                ),
                whole(seg_col.shape),
                pl.BlockSpec((1, BLOCK), lambda i, lo, hi, pos: (0, i)),
            ]
            + [pl.BlockSpec(memory_space=pl.ANY)] * len(ready),
            out_specs=(
                pl.BlockSpec((BLOCK, LANES), lambda i, lo, hi, pos: (pos[i], 0)),
                whole(rows_out.shape),
                whole(rows_out.shape),
                whole(offsets.shape),
            ),
            scratch_shapes=[
                pltpu.VMEM((LANES, BLOCK), F32),
                pltpu.VMEM((seq_length, LANES), F32),
                pltpu.VMEM((seq_length, LANES), F32),
                pltpu.VMEM((count, diags, BLOCK, BLOCK), F32),
            ],
        ),
        compiler_params=params(),
        cost_estimate=cost(2.2e10 * count, 5e6 * count),
        name="attend_back",
    )(*spans, qkv, grad_heads, head_out, norms, qkv, key_t, qkv, tiles, seg_col, seg_row, *ready)


def split_rows(refs):
    parts = [r[...].reshape(-1, r.shape[-1]) for r in refs]
    return jnp.concatenate(parts, axis=0)


def store_rows(refs, values):
    size = values.shape[0] // len(refs)
    for n, r in enumerate(refs):
        r[...] = values[n * size : (n + 1) * size].astype(r.dtype).reshape(r.shape)


def expert_kernel(groups, *refs):
    xs, us = refs[:groups], refs[groups : 2 * groups]
    win_ref, wout_ref, wr_ref, hot_ref = refs[2 * groups : 2 * groups + 4]
    outs = refs[2 * groups + 4 : 3 * groups + 4]
    act_ref, gpre_ref, gu_ref, gl_ref = refs[3 * groups + 4 :]
    hot = hot_ref[0]
    size = act_ref.shape[2] // 2
    for n in range(2):
        part = slice(n * groups // 2, (n + 1) * groups // 2)
        rows = slice(n * size, (n + 1) * size)
        x = split_rows(xs[part])
        u = split_rows(us[part])
        logits = dot_nn(x, wr_ref[...])
        powers = jnp.exp(logits - jnp.max(logits, axis=-1, keepdims=True))
        probs = powers / jnp.sum(powers, axis=-1, keepdims=True)
        gate = jnp.sum(probs * hot, axis=-1, keepdims=True)
        pre = dot_nn(x, win_ref[0])
        back = dot_nt(u, wout_ref[0])
        square = pre * pre
        bent = jnp.tanh(pre * (GELU_A + GELU_A * GELU_B * square))
        half = 0.5 + 0.5 * bent
        act = (pre * half).astype(BF16)
        slope = half + pre * (0.5 - 0.5 * bent * bent) * (GELU_A + 3.0 * GELU_A * GELU_B * square)
        grad_gate = jnp.sum(act.astype(F32) * back, axis=-1, keepdims=True)
        grad_pre = (gate * back * slope).astype(BF16)
        grad_logits = grad_gate * gate * (hot - probs)
        high = grad_logits.astype(BF16)
        rest = (grad_logits - high.astype(F32)).astype(BF16)
        grad_x = dot_nt(grad_pre, win_ref[0]) + dot_nt(high, wr_ref[...])
        store_rows(outs[part], grad_x + dot_nt(rest, wr_ref[...]))
        act_ref[0, 0, rows] = act
        gpre_ref[0, 0, rows] = grad_pre
        gu_ref[0, 0, rows] = (gate * u.astype(F32)).astype(BF16)
        gl_ref[0, 0, rows] = grad_logits


def slot_specs(groups, tile, capacity, width, first=0):
    spec = pl.BlockSpec((tile, 1, capacity, width), lambda e, t: (t, e + first, 0, 0))
    return [spec] * groups


def experts(xs, us, w_in, w_out, w_router, hots, first):
    groups = len(xs)
    sources, count, capacity, width = xs[0].shape
    tile = min(sources, DIRECT)
    tiles = sources // tile
    rows = groups * tile * capacity
    hidden_units = w_in.shape[2]
    slots = slot_specs(groups, tile, capacity, width)
    kept = lambda last: pl.BlockSpec((1, 1, rows, last), lambda e, t: (e, t, 0, 0))
    kept_shape = lambda last, dt: jax.ShapeDtypeStruct((count, tiles, rows, last), dt)
    expert_count = w_router.shape[1]
    res = pl.pallas_call(
        lambda *refs: expert_kernel(groups, *refs),
        out_shape=[jax.ShapeDtypeStruct(xs[0].shape, BF16)] * groups
        + [
            kept_shape(hidden_units, BF16),
            kept_shape(hidden_units, BF16),
            kept_shape(width, BF16),
            kept_shape(expert_count, F32),
        ],
        grid=(count, tiles),
        in_specs=slots
        + slot_specs(groups, tile, capacity, width, first)
        + [
            pl.BlockSpec((1, width, hidden_units), lambda e, t: (e + first, 0, 0)),
            pl.BlockSpec((1, hidden_units, width), lambda e, t: (e + first, 0, 0)),
            pl.BlockSpec(w_router.shape, lambda e, t: (0, 0)),
            pl.BlockSpec((1, 1, expert_count), lambda e, t: (e + first, 0, 0)),
        ],
        out_specs=slots + [kept(hidden_units), kept(hidden_units), kept(width), kept(expert_count)],
        compiler_params=params(),
        cost_estimate=cost(17 * count * tiles * rows * width * hidden_units, 7e6 * count),
        name="experts",
    )(*xs, *us, w_in, w_out, w_router, hots)
    return res[:groups], res[groups:]


def weight_kernel(groups, *refs):
    xs = refs[:groups]
    act_ref, gpre_ref, gu_ref, gl_ref, wout_ref = refs[groups : groups + 5]
    outs = refs[-groups - 3 : -3]
    gin_ref, gout_ref, gr_ref = refs[-3:]
    x = split_rows(xs)
    act = act_ref[0, 0]
    store_rows(outs, dot_nn(act, wout_ref[0]))
    grad_logits = gl_ref[0, 0]
    high = grad_logits.astype(BF16)
    rest = (grad_logits - high.astype(F32)).astype(BF16)
    first = pl.program_id(1) == 0

    @pl.when(first)
    def _():
        gin_ref[0] = dot_tn(x, gpre_ref[0, 0])
        gout_ref[0] = dot_tn(act, gu_ref[0, 0])

    @pl.when(jnp.logical_not(first))
    def _():
        gin_ref[0] += dot_tn(x, gpre_ref[0, 0])
        gout_ref[0] += dot_tn(act, gu_ref[0, 0])

    router = dot_tn(x, high) + dot_tn(x, rest)
    start = first & (pl.program_id(0) == 0)

    @pl.when(start)
    def _():
        gr_ref[...] = router

    @pl.when(jnp.logical_not(start))
    def _():
        gr_ref[...] += router


def expert_weights(xs, kept, w_out, first, earlier):
    groups = len(xs)
    sources, count, capacity, width = xs[0].shape
    tile = min(sources, DIRECT)
    tiles = sources // tile
    rows = groups * tile * capacity
    hidden_units = w_out.shape[1]
    expert_count = kept[3].shape[-1]
    slots = slot_specs(groups, tile, capacity, width)
    held = lambda last: pl.BlockSpec((1, 1, rows, last), lambda e, t: (e, t, 0, 0))
    anywhere = [pl.BlockSpec(memory_space=pl.ANY)] * len(earlier)
    inputs = groups + 5
    res = pl.pallas_call(
        lambda *refs: weight_kernel(groups, *refs),
        out_shape=[jax.ShapeDtypeStruct((sources, w_out.shape[0], capacity, width), BF16)] * groups
        + [
            jax.ShapeDtypeStruct((w_out.shape[0], width, hidden_units), F32),
            jax.ShapeDtypeStruct((w_out.shape[0], hidden_units, width), F32),
            jax.ShapeDtypeStruct((width, expert_count), F32),
        ],
        grid=(count, tiles),
        in_specs=slots
        + [held(hidden_units), held(hidden_units), held(width), held(expert_count)]
        + [pl.BlockSpec((1, hidden_units, width), lambda e, t: (e + first, 0, 0))]
        + anywhere,
        out_specs=slot_specs(groups, tile, capacity, width, first)
        + [
            pl.BlockSpec((1, width, hidden_units), lambda e, t: (e + first, 0, 0)),
            pl.BlockSpec((1, hidden_units, width), lambda e, t: (e + first, 0, 0)),
            pl.BlockSpec((width, expert_count), lambda e, t: (0, 0)),
        ],
        input_output_aliases={inputs + n: n for n in range(len(earlier))},
        compiler_params=params(),
        cost_estimate=cost(17 * count * tiles * rows * width * hidden_units, 1e7 * count),
        name="expert_weights",
    )(*xs, *kept, w_out, *earlier)
    return res[: groups + 2], res[groups + 2]


def after(values, *earlier):
    return lax.optimization_barrier((values,) + earlier)[0]


def swap(values, axis, step):
    count = lax.axis_size(axis)
    return lax.ppermute(values, axis, [(n, n ^ step) for n in range(count)])


def gather_mp(values):
    across = swap(values, "mp", 2)
    return [values, swap(values, "mp", 1), across, swap(across, "mp", 1)]


def fold_mp(parts):
    near = parts[0].astype(F32) + swap(parts[1], "mp", 1).astype(F32)
    far = parts[2].astype(F32) + swap(parts[3], "mp", 1).astype(F32)
    return near + swap(far.astype(BF16), "mp", 2).astype(F32)


def unless_nan(values, flag):
    return jnp.where(flag != flag, jnp.zeros_like(values), values)


def trade_dp(values):
    return lax.all_to_all(values, "dp", split_axis=0, concat_axis=0, tiled=True)


def trade_dp_steps(values):
    count = lax.axis_size("dp")
    if count > DIRECT:
        return trade_dp(values)
    own = lax.axis_index("dp")
    held, step = values[None], count // 2
    while step > 0:
        low = (own // step) % 2 == 0
        sent, size = held.shape[0], held.shape[1] // 2
        first, second = held[:, :size], held[:, size:]
        leave = jnp.where(low, second, first)
        came = swap(leave, "dp", step)
        stay = jnp.where(low, first, second)
        held = jnp.stack([jnp.where(low, stay, came), jnp.where(low, came, stay)], axis=1)
        held = held.reshape((2 * sent, size) + values.shape[1:])
        step //= 2
    return held[:, 0]


def sum_steps(values, axis):
    step = 1
    while step < lax.axis_size(axis):
        values = values + swap(values, axis, step)
        step *= 2
    return values


def fold_dp(values):
    count = lax.axis_size("dp")
    parts = values.reshape((count, values.shape[0] // count) + values.shape[1:])
    return jnp.sum(trade_dp(parts).astype(F32), axis=0)


def share_dp(pieces):
    mine = jnp.concatenate(pieces, axis=1).astype(BF16)
    count = lax.axis_size("dp")
    whole = trade_dp(jnp.broadcast_to(mine[None], (count,) + mine.shape))
    whole = whole.reshape(-1, mine.shape[1]).astype(F32)
    ends = [0]
    for p in pieces:
        ends.append(ends[-1] + p.shape[1])
    return [whole[:, a:b] for a, b in zip(ends, ends[1:])]


def per_device(
    tokens,
    cotangent,
    norm1_gain,
    w_query,
    w_key,
    w_value,
    w_attn_out,
    bias_table,
    norm2_gain,
    w_router,
    w_expert_in,
    w_expert_out,
    routes,
    segments,
    buckets,
):
    tok_rows, model_width = tokens.shape
    groups = lax.axis_size("mp")
    sources = lax.axis_size("dp")
    own_mp, own_dp = lax.axis_index("mp"), lax.axis_index("dp")
    seq_length = tok_rows * groups
    blocks = seq_length // BLOCK
    bucket_count, heads_local = bias_table.shape
    head_width = w_query.shape[1]
    expert_count = w_router.shape[1]
    capacity = 2 * tok_rows // expert_count
    exp_local = w_expert_in.shape[0]
    chunks = 2 if exp_local % 2 == 0 else 1
    chunk_experts = exp_local // chunks
    reach = min(LONGEST // BLOCK, blocks - 1)
    head_dim = head_width // heads_local
    lane_groups = -(-head_width // LANES)

    inputs = tokens.astype(F32)
    scale_one = rms_scale(inputs)
    normed_one = (inputs * scale_one * norm1_gain).astype(BF16)
    half = tok_rows // 2
    pieces = zip(gather_mp(normed_one[:half]), gather_mp(normed_one[half:]))
    normed_all = jnp.concatenate([part for pair in pieces for part in pair], axis=0)

    expert_of = routes[:, 0]
    chosen = expert_of[:, None] == jnp.arange(expert_count, dtype=jnp.int32)[None, :]
    positions = jnp.arange(tok_rows, dtype=jnp.int32)
    earlier = (positions[None, :] < positions[:, None]).astype(BF16)
    before = jnp.dot(earlier, chosen.astype(BF16), preferred_element_type=F32)
    slot_rank = jnp.sum(before * chosen.astype(F32), axis=-1).astype(jnp.int32)
    slot_index = expert_of * capacity + slot_rank
    slot_count = expert_count * capacity
    picks = (slot_index[:, None] == jnp.arange(slot_count, dtype=jnp.int32)[None, :]).astype(BF16)

    def to_slots(rows):
        slots = dot_tn(picks, rows).astype(BF16)
        return slots.reshape(sources, exp_local, capacity, model_width)

    offsets = jnp.concatenate([buckets[::-1], jnp.full((1,), -1, jnp.int32)])
    first = seq_length - (reach + 1) * BLOCK
    offsets = offsets[first : first + (2 * reach + 2) * BLOCK]
    bucket_hot = (
        offsets[None, :] == jnp.arange(bucket_count, dtype=jnp.int32)[:, None]
    ).astype(F32)
    bias_rows = jnp.dot(bias_table.T, bucket_hot, precision=PRECISE)
    tiles = bias_tiles(bias_rows[:, None, :], 2 * reach + 1)

    seg_all = segments[0]
    ends = seg_all.reshape(blocks, BLOCK)
    low = jnp.sum(seg_all[None, :] < ends[:, :1], axis=1, dtype=jnp.int32) // BLOCK
    high = -(-jnp.sum(seg_all[None, :] <= ends[:, -1:], axis=1, dtype=jnp.int32) // BLOCK)
    block_ids = jnp.arange(blocks, dtype=jnp.int32)
    low = jnp.maximum(low, block_ids - reach)
    high = jnp.minimum(high, block_ids + reach + 1)
    per = tok_rows // BLOCK
    spans = (low, high, (block_ids // per ^ own_mp) * per + block_ids % per)
    seg_col, seg_row = seg_all[:, None], seg_all[None, :]

    up_slots = trade_dp(to_slots(after(cotangent, normed_one)))

    spare = ((0, 0), (0, lane_groups * LANES - head_width))
    padded = [jnp.pad(w, spare) for w in (w_query, w_key, w_value)]
    scaled = jnp.concatenate([padded[0] * jnp.asarray(SCORE_SCALE, BF16)] + padded[1:], axis=1)
    qkv = jnp.dot(normed_all, scaled, preferred_element_type=F32).astype(BF16)
    value_t = qkv[:, 2 * padded[0].shape[1] :].T
    grad_slots = gather_mp(after(up_slots, normed_all))
    w_out_parts = gather_mp(after(w_attn_out, normed_all))
    head_out, norms = attend(
        qkv, value_t, tiles, seg_col, seg_row, spans, heads_local, head_dim
    )

    def block_of(rows, n):
        return rows[n * tok_rows : (n + 1) * tok_rows]

    head_rows = head_out[:, :head_width]
    head_parts = [block_of(head_rows, 0)] + [
        swap(block_of(head_rows, n), "mp", n) for n in range(1, groups)
    ]
    attn = jnp.dot(
        jnp.concatenate(head_parts, axis=1),
        jnp.concatenate(w_out_parts, axis=0),
        preferred_element_type=F32,
    )
    hidden = inputs + attn
    scale_two = rms_scale(hidden)
    normed_two = (hidden * scale_two * norm2_gain).astype(BF16)
    slots = trade_dp(to_slots(normed_two))
    token_slots = [
        gather_mp(slots[:, c * chunk_experts : (c + 1) * chunk_experts]) for c in range(chunks)
    ]

    hots = (
        (own_dp * exp_local + jnp.arange(exp_local, dtype=jnp.int32))[:, None]
        == jnp.arange(expert_count, dtype=jnp.int32)[None, :]
    ).astype(F32)[:, None, :]
    folded, kept = [], []
    for c in range(chunks):
        parts, extra = experts(
            token_slots[c], grad_slots, w_expert_in, w_expert_out, w_router, hots,
            c * chunk_experts,
        )
        folded.append(fold_mp(parts).astype(BF16))
        kept.append(extra)
    back = [trade_dp(f) for f in folded]
    grad_w_router, made = 0.0, ()
    for c in range(chunks):
        made, grad_router = expert_weights(
            token_slots[c], kept[c], w_expert_out, c * chunk_experts, made
        )
        grad_w_router = grad_w_router + grad_router
    grad_w_expert_in, grad_w_expert_out = made[groups:]
    far_rows = (made[2].astype(F32) + swap(made[3], "mp", 1).astype(F32)).astype(BF16)
    near_rows = made[0].astype(F32) + swap(made[1], "mp", 1).astype(F32)
    back = jnp.concatenate(back, axis=1).reshape(-1, model_width)
    grad_normed_two = jnp.dot(picks, after(back, grad_w_router), preferred_element_type=F32)

    upstream = cotangent.astype(F32)
    grad_hidden, grad_norm2_gain = norm_back(hidden, scale_two, norm2_gain, grad_normed_two)
    grad_hidden = grad_hidden + upstream
    grad_attn = grad_hidden.astype(BF16)

    grad_heads = [dot_nt(grad_attn, w).astype(BF16) for w in w_out_parts]
    grad_heads = [g if n == 0 else swap(g, "mp", n) for n, g in enumerate(grad_heads)]
    grad_heads = jnp.pad(jnp.concatenate(grad_heads, axis=0), spare)
    key_t = qkv[:, padded[0].shape[1] : 2 * padded[0].shape[1]].T

    shared = jnp.concatenate([grad_w_router, grad_norm2_gain[:, None]], axis=1)
    shared = sum_steps(after(shared, grad_attn), "mp")
    grad_attn_all = jnp.concatenate(gather_mp(after(grad_attn, grad_heads)), axis=0)
    rest = [dot_tn(grad_attn_all, head_rows), shared]
    folded_rows = (near_rows + swap(far_rows, "mp", 2).astype(F32)).astype(BF16)
    order, piece_of, bias_sums, gain_sum, summed = [], [], [], 0.0, []
    ready = [far_rows]
    for g in range(lane_groups):
        grad_q, grad_k, grad_v, offset_grad = attend_back(
            g, heads_local, head_dim, qkv, grad_heads, head_out, norms, key_t, tiles, seg_col,
            seg_row, spans, ready,
        )
        lanes = min(LANES, head_width - g * LANES)
        own = jnp.concatenate([grad_q, grad_k, grad_v], axis=1)
        weights = jnp.concatenate([w[:, g * LANES : (g + 1) * LANES] for w in padded], axis=1)
        order.append((own, weights))
        partial = dot_tn(normed_all, own)
        gain_sum = gain_sum + jnp.sum(partial * weights.astype(F32), axis=1)
        partial = [partial[:, n * LANES : n * LANES + lanes] for n in range(3)]
        payload = jnp.concatenate(partial + rest, axis=1).astype(BF16)
        if summed:
            payload = unless_nan(payload, summed[-1][0, 0])
        piece_of.append((lanes, payload.shape[1]))
        rest, ready = [], [payload, folded_rows]
        summed.append(fold_dp(payload))
        bias_sums.append(offset_grad[: lanes // head_dim])
    summed = share_dp(summed)
    grads = [[], [], []]
    for (lanes, _), columns in zip(piece_of, summed):
        for n in range(3):
            grads[n].append(columns[:, n * lanes : (n + 1) * lanes])
    grads = [jnp.concatenate(g, axis=1) for g in grads]
    rest = summed[0][:, 3 * piece_of[0][0] :]
    grad_w_attn_out, shared = rest[:, :head_width].T, rest[:, head_width:]

    rows_back = trade_dp_steps(folded_rows)
    router_logits = jnp.dot(normed_two, w_router, preferred_element_type=F32)
    router_exp = jnp.exp(router_logits - jnp.max(router_logits, axis=-1, keepdims=True))
    router_probs = router_exp / jnp.sum(router_exp, axis=-1, keepdims=True)
    gate_prob = jnp.sum(router_probs * chosen.astype(F32), axis=-1, keepdims=True)
    expert_rows = jnp.dot(picks, rows_back.reshape(-1, model_width), preferred_element_type=F32)
    mixed = (hidden + gate_prob * expert_rows).astype(BF16)

    own = jnp.concatenate([p[0] for p in order], axis=1)
    weights = jnp.concatenate([p[1] for p in order], axis=1)
    total = dot_nt(own, weights).astype(BF16)
    grad_normed_one = fold_mp([block_of(total, n) for n in range(groups)])
    bias_sums = jnp.dot(jnp.concatenate(bias_sums, axis=0), bucket_hot.T, precision=PRECISE)
    small = jnp.concatenate([gain_sum / norm1_gain, bias_sums.reshape(-1)])
    small = jnp.pad(small, (0, -small.shape[0] % (8 * LANES))).reshape(8, -1)
    small = sum_steps(small, "dp")
    grad_norm1_gain = sum_steps(small, "mp").reshape(-1)[:model_width]
    bias_sums = small.reshape(-1)[model_width : model_width + heads_local * bucket_count]
    grad_bias_table = bias_sums.reshape(heads_local, -1).T
    weighted = norm1_gain * grad_normed_one
    grad_inputs = scale_one * weighted - inputs * scale_one * scale_one * scale_one * jnp.mean(
        weighted * inputs, axis=-1, keepdims=True
    )
    grad_tokens = (grad_inputs + grad_hidden).astype(BF16)
    return (
        mixed,
        grad_tokens,
        grad_norm1_gain,
        *grads,
        grad_w_attn_out,
        grad_bias_table,
        shared[:, expert_count],
        shared[:, :expert_count],
        grad_w_expert_in,
        grad_w_expert_out,
    )


def solution(mesh):
    return jax.shard_map(
        per_device,
        mesh=mesh,
        in_specs=(
            P(("dp", "mp"), None),
            P(("dp", "mp"), None),
            P(),
            P(None, "mp"),
            P(None, "mp"),
            P(None, "mp"),
            P("mp", None),
            P(None, "mp"),
            P(),
            P(),
            P("dp", None, "mp"),
            P("dp", "mp", None),
            P(("dp", "mp"), None),
            P("dp", None),
            P(),
        ),
        out_specs=(
            P(("dp", "mp"), None),
            P(("dp", "mp"), None),
            P(),
            P(None, "mp"),
            P(None, "mp"),
            P(None, "mp"),
            P("mp", None),
            P(None, "mp"),
            P(),
            P(),
            P("dp", None, "mp"),
            P("dp", "mp", None),
        ),
        check_vma=False,
    )
```
